512 devices in a mesh: dp: 128 (over z, y, core), grp: 4 (over x).
Axes of the slice: x: 4, y: 8, z: 8, core: 2. Of those that a mesh axis runs over, the one named last changes fastest.
Arguments:
- features: bfloat16 [65536, 512], P(('dp', 'grp'))
- loss_scale: bfloat16 [65536], P(('dp', 'grp')), may hold values from 8 to 32
- blocks: int32 [65536, 8], P(('dp', 'grp')), may hold values from 0 to 511, all different within a row; in each aligned block of 128 rows (0 to 127, 128 to 255, ...) at most 3 rows name the same one
- label_col: int32 [65536], P(('dp', 'grp')), may hold values from 0 to 1023
- block_slot: int32 [512], replicated, may hold values from 0 to 511, each once
- centers: bfloat16 [524288, 512], P(('dp', 'grp'))
Outputs:
- loss_out: float32 [65536], P(('dp', 'grp'))
- feature_grad: float32 [65536, 512], P(('dp', 'grp'))
- center_grad: bfloat16 [524288, 512], P(('dp', 'grp'))
The draws below stay inside these ranges and needn't reach their ends.
Inputs may be any that keep to these rules, and one draw needn't show every extreme that they name: Each row names 8 different blocks; the first is the sample's own block. Among the rows of one device no block is named by more than 3 rows, and some block is named by exactly 3. A permutation: block b is stored in rows block_slot[b] * 1024 to block_slot[b] * 1024 + 1023 of centers.
All inputs are finite; a program needn't handle non-finite values.
Results may differ from the reference program's by a relative error of at most 0.0054.
Values may be sent and summed in bfloat16 or wider, within the bound.
No kernel may reach another device: no remote copies, remote signals or barrier semaphores. Data moves between devices by JAX's collectives and lax.ppermute only.
A program may use at most 64 MiB of HBM per device.

```python
import math
import jax
import jax.numpy as jnp
import numpy as np
from jax import lax

E = 512
BLOCK = 1024
PICKS = 8
TOK_DEV = 128
NB = 512
SAMPLES = 65536
MOST = 3
CAPB = 1536


def draw_features(key, part):
    base = jax.random.normal(jax.random.fold_in(key, 1), (SAMPLES, E), jnp.float32)
    spread = jnp.exp(jax.random.uniform(jax.random.fold_in(key, 2), (SAMPLES, 1), jnp.float32, jnp.log(2.0), jnp.log(16.0)))
    return (base * spread).astype(jnp.bfloat16)


def draw_centers(key, part):
    base = jax.random.normal(jax.random.fold_in(key, 5), (NB * BLOCK, E), jnp.float32)
    return base.astype(jnp.bfloat16)


def touch_ends(values, key, least, largest):
    longest = values.shape.index(max(values.shape))
    spots = []
    for shift in (0, 1):
        where = [jax.random.randint(jax.random.fold_in(key, axis), (), 0, length) for axis, length in enumerate(values.shape)]
        where[longest] = (where[longest] + shift) % values.shape[longest]
        spots.append(tuple(where))
    return values.at[spots[0]].set(least).at[spots[1]].set(largest)


def levels(own_key, dims, split, least, top_value):
    def one(dim, blocks):
        heights = jax.random.uniform(jax.random.fold_in(jax.random.fold_in(own_key, 6), dim), (blocks,), jnp.float32, least / len(split), top_value / len(split))
        return jnp.repeat(jnp.exp(heights), dims[dim] // blocks).reshape((-1,) + (1,) * (len(dims) - dim - 1))

    gain = one(*split[0])
    for cut in split[1:]:
        gain = gain * one(*cut)
    return gain


def routed_block(key, own, number, rows, count, top, most, skew):
    order = jax.random.permutation(key, count)
    packed, common = portions_of(count, rows * top, most, skew, True), portions_of(count, rows * top, most, skew, False)
    places = jnp.arange(count)

    def named(tallies, turn):
        used = int((tallies > 0).sum())
        fixed = max(1, used // 4)
        moved = fixed + (places - fixed + turn * (used - fixed)) % max(1, count - fixed)
        return jnp.zeros((count,), jnp.int32).at[order[jnp.where(places < fixed, places, moved)]].set(jnp.asarray(tallies, jnp.int32))

    tallies = jnp.where(number % 4 == 0, named(packed, number // 4), named(common, number - number // 4 - 1))
    mixed = jax.random.permutation(jax.random.fold_in(own, 3), count)
    donor, receiver = mixed[0:count // 2 * 2:2], mixed[1:count // 2 * 2:2]
    margin = jnp.minimum(tallies[donor] - 1, most - tallies[receiver]) // 2
    margin = jnp.where((donor == order[0]) | (receiver == order[0]) | (tallies[receiver] == 0), 0, jnp.maximum(margin, 0))
    moved = jax.random.randint(jax.random.fold_in(own, 4), (count // 2,), 0, 1 << 20) % (margin + 1)
    tallies = tallies.at[donor].add(-moved).at[receiver].add(moved)
    members = jnp.searchsorted(jnp.cumsum(tallies), jnp.arange(rows * top), side="right").astype(jnp.int32)
    grid = members.reshape(top, rows).T
    grid = grid[jax.random.permutation(jax.random.fold_in(own, 1), rows)]
    turn = jax.random.randint(jax.random.fold_in(own, 2), (rows, 1), 0, top)
    return jnp.take_along_axis(grid, (jnp.arange(top)[None, :] + turn) % top, axis=1)


def portions_of(number_of, total, most, slope, full):
    portions = [(1 << 20) // math.isqrt(grade ** slope) + 1 for grade in range(1, number_of + 1)]
    largest = most if full else min(most, max(-(-total // number_of), total * portions[0] // sum(portions)))
    least = 1 if total - largest >= number_of - 1 else 0
    counts, rest = [largest] + [least] * (number_of - 1), total - largest - least * (number_of - 1)
    while rest > 0:
        movable = [i for i in range(1, number_of) if counts[i] < largest] or [i for i in range(1, number_of) if counts[i] < most]
        pool, budget = sum([portions[i] for i in movable]), rest
        for i in movable:
            more = min(most - counts[i], max(1, budget * portions[i] // pool), rest)
            counts[i] = counts[i] + more
            rest = rest - more
    return np.array(counts)


def setup_inputs(seed: int = 0) -> dict:
    keys = jax.random.split(jax.random.key(seed), 7)
    features = draw_features(jax.random.fold_in(keys[6], 71), 0)
    loss_scale = jnp.clip(jnp.exp(math.log(32.0) - 1.3862944 * jax.random.uniform(keys[1], (SAMPLES,), jnp.float32) ** levels(keys[1], (SAMPLES,), ((0, 512),), -0.2, 0.2)), 8.0, 32.0).astype(jnp.bfloat16)
    blocks_keys = jax.random.split(jax.random.fold_in(keys[2], 1), SAMPLES // TOK_DEV)
    blocks_turns = jax.random.permutation(jax.random.fold_in(keys[2], 3), SAMPLES // TOK_DEV)
    blocks = jax.vmap(lambda own, number: routed_block(jax.random.fold_in(keys[2], 2), own, number, TOK_DEV, NB, PICKS, MOST, 2))(blocks_keys, blocks_turns).reshape((SAMPLES, PICKS))
    label_col = touch_ends(jax.random.randint(keys[3], (SAMPLES,), 0, BLOCK), jax.random.fold_in(keys[3], 1), 0, BLOCK - 1).astype(jnp.int32)
    block_slot = jax.random.permutation(keys[4], NB).astype(jnp.int32)
    centers = draw_centers(jax.random.fold_in(keys[6], 71), 0)
    return {"features": features, "loss_scale": loss_scale, "blocks": blocks, "label_col": label_col, "block_slot": block_slot, "centers": centers}


MARGIN = 0.35
LOGIT_SCALE = 64.0
EPSILON = 1e-06
FLOOR_MAX = -1e+30

def normalize(block_w):
    widened = block_w.astype(jnp.float32)
    lengths = jnp.sqrt(lax.optimization_barrier(jnp.sum(widened * widened, axis=1)) + EPSILON)
    unit_rows = widened / lengths[:, None]
    return (unit_rows.astype(jnp.bfloat16), unit_rows, lengths)

def block_logits(rows_x, normed, columns):
    scores = lax.dot_general(rows_x, normed, (((1,), (1,)), ((), ())), preferred_element_type=jnp.float32)
    positive = lax.broadcasted_iota(jnp.int32, scores.shape, 1) == columns[:, None]
    scores = LOGIT_SCALE * scores - jnp.where(positive, LOGIT_SCALE * MARGIN, 0.0)
    return (scores, positive)

def center_terms(scores, positive, rows_x, normed, unit_rows, lengths, gains, is_valid, row_peak, row_denom):
    probs_row = jnp.exp(scores - row_peak[:, None]) / row_denom[:, None]
    weights = gains.astype(jnp.float32)[:, None] * (probs_row - positive.astype(jnp.float32))
    weights = jnp.where(is_valid[:, None], weights, 0.0).astype(jnp.bfloat16)
    returned = LOGIT_SCALE * jnp.dot(weights, normed, preferred_element_type=jnp.float32)
    unit_grad = LOGIT_SCALE * lax.dot_general(weights, rows_x, (((0,), (0,)), ((), ())), preferred_element_type=jnp.float32)
    along_unit = lax.optimization_barrier(jnp.sum(unit_rows * unit_grad, axis=1, keepdims=True))
    grad_rows = ((unit_grad - unit_rows * along_unit) / lengths[:, None]).astype(jnp.bfloat16)
    return (returned, grad_rows)

def pair_table(blocks, label_col, block_slot):
    pair_count = SAMPLES * PICKS
    pair_iota = jnp.arange(pair_count, dtype=jnp.int32)
    sample_ids = pair_iota // PICKS
    pick_ids = pair_iota % PICKS
    flat_blocks = blocks.reshape(-1).astype(jnp.int32)
    source = sample_ids // TOK_DEV
    within = sample_ids % TOK_DEV
    sort_keys = (source * NB + flat_blocks) * TOK_DEV + within
    ordering = jnp.argsort(sort_keys, stable=True).astype(jnp.int32)
    sorted_groups = sort_keys[ordering] // TOK_DEV
    starts = jnp.concatenate([jnp.ones((1,), bool), sorted_groups[1:] != sorted_groups[:-1]])
    group_start = lax.cummax(jnp.where(starts, pair_iota, 0), axis=0)
    rank_of = jnp.zeros((pair_count,), jnp.int32).at[ordering].set(pair_iota - group_start)
    slot_ids = block_slot[flat_blocks].astype(jnp.int32)
    index = slot_ids * CAPB + source * MOST + rank_of
    ids_table = jnp.full((NB * CAPB,), SAMPLES, jnp.int32).at[index].set(sample_ids)
    col_values = jnp.where(pick_ids == 0, label_col[sample_ids].astype(jnp.int32), -1)
    col_table = jnp.full((NB * CAPB,), -1, jnp.int32).at[index].set(col_values)
    return (ids_table.reshape(NB, CAPB), col_table.reshape(NB, CAPB))

def reference(features, loss_scale, blocks, label_col, block_slot, centers):
    ids_table, col_table = pair_table(blocks, label_col, block_slot)
    normed_feat, unit_feat, feat_norm = normalize(features)
    padded = jnp.concatenate([normed_feat, jnp.zeros((1, E), jnp.bfloat16)])
    scales = jnp.concatenate([loss_scale.astype(jnp.float32), jnp.zeros((1,), jnp.float32)])
    blocks_w = centers.reshape(NB, BLOCK, E)

    def first_pass(slot_idx):
        row_ids = ids_table[slot_idx]
        normed, unit_rows, lengths = normalize(blocks_w[slot_idx])
        scores, positive = block_logits(padded[row_ids], normed, col_table[slot_idx])
        highest = lax.optimization_barrier(jnp.max(scores, axis=1))
        totals = lax.optimization_barrier(jnp.sum(jnp.exp(scores - highest[:, None]), axis=1))
        picked = lax.optimization_barrier(jnp.sum(jnp.where(positive, scores, 0.0), axis=1))
        return (highest, totals, picked)
    highs, totals, picks = lax.map(first_pass, jnp.arange(NB, dtype=jnp.int32))
    flat_ids = ids_table.reshape(-1)
    highs = highs.reshape(-1)
    sample_peak = jnp.full((SAMPLES + 1,), FLOOR_MAX, jnp.float32).at[flat_ids].max(highs)
    sample_denom = jnp.zeros((SAMPLES + 1,), jnp.float32).at[flat_ids].add(totals.reshape(-1) * jnp.exp(highs - sample_peak[flat_ids]))
    target = jnp.zeros((SAMPLES + 1,), jnp.float32).at[flat_ids].add(picks.reshape(-1))
    loss_all = sample_peak + jnp.log(sample_denom) - target

    def second_pass(grad_acc, slot_idx):
        row_ids = ids_table[slot_idx]
        normed, unit_rows, lengths = normalize(blocks_w[slot_idx])
        rows_x = padded[row_ids]
        scores, positive = block_logits(rows_x, normed, col_table[slot_idx])
        returned, grad_rows = center_terms(scores, positive, rows_x, normed, unit_rows, lengths, scales[row_ids], row_ids < SAMPLES, sample_peak[row_ids], sample_denom[row_ids])
        return (grad_acc.at[row_ids].add(returned), grad_rows)
    grad_init = jnp.zeros((SAMPLES + 1, E), jnp.float32)
    grad_acc, center_rows = lax.scan(second_pass, grad_init, jnp.arange(NB, dtype=jnp.int32))
    unit_fgrad = grad_acc[:SAMPLES]
    along = lax.optimization_barrier(jnp.sum(unit_feat * unit_fgrad, axis=1, keepdims=True))
    feature_grad = (unit_fgrad - unit_feat * along) / feat_norm[:, None]
    return (loss_all[:SAMPLES], feature_grad, center_rows.reshape(NB * BLOCK, E))
```

```python
import jax
import jax.numpy as jnp
from jax import lax
from jax.experimental import pallas as pl
from jax.experimental.pallas import tpu as pltpu
from jax.sharding import PartitionSpec as P

BLOCK = 1024
MOST = 3
LANES = 128
MARGIN = 0.35
LOGIT_SCALE = 64.0
EPSILON = 1e-06
AXES = ("dp", "grp")

VMEM = pl.BlockSpec(memory_space=pltpu.VMEM)


def nt_dot(a, b):
    return lax.dot_general(a, b, (((1,), (1,)), ((), ())), preferred_element_type=jnp.float32)


def tn_dot(a, b):
    return lax.dot_general(a, b, (((0,), (0,)), ((), ())), preferred_element_type=jnp.float32)


def nn_dot(a, b):
    return jnp.dot(a, b, preferred_element_type=jnp.float32)


def call(kernel, outs, scratch=(), name=None):
    return pl.pallas_call(
        kernel,
        out_shape=outs,
        scratch_shapes=list(scratch),
        compiler_params=pltpu.CompilerParams(vmem_limit_bytes=56 * 1024 * 1024),
        name=name,
    )


def dispatch_kernel(feat_ref, blocks_ref, label_ref, slot_ref, pay_ref, sel_ref, stage):
    samples, width = feat_ref.shape
    total = slot_ref.shape[1]
    segs = width // LANES
    rows = MOST * segs + 2
    x = feat_ref[...].astype(jnp.float32)
    norm = jnp.sqrt(jnp.sum(x * x, axis=1, keepdims=True) + EPSILON)
    normed = (x / norm).astype(jnp.bfloat16)
    named_by = blocks_ref[...]
    block_iota = lax.broadcasted_iota(jnp.int32, (samples, total), 1)
    own = named_by[:, 0:1] == block_iota
    named = own
    for k in range(1, blocks_ref.shape[1]):
        named = named | (named_by[:, k : k + 1] == block_iota)
    one_hot = (lax.broadcasted_iota(jnp.int32, (total, total), 0) == slot_ref[...]).astype(
        jnp.float32
    ).astype(jnp.bfloat16)
    named_at = nt_dot(one_hot, named.astype(jnp.float32).astype(jnp.bfloat16))
    own_at = nt_dot(one_hot, own.astype(jnp.float32).astype(jnp.bfloat16))
    before = (
        lax.broadcasted_iota(jnp.int32, (samples, samples), 0)
        < lax.broadcasted_iota(jnp.int32, (samples, samples), 1)
    ).astype(jnp.float32).astype(jnp.bfloat16)
    rank = nn_dot(named_at.astype(jnp.bfloat16), before)
    label = label_ref[...].astype(jnp.float32) + 1.0
    own_label = own_at * label
    lane = lax.broadcasted_iota(jnp.int32, (total, LANES), 1)
    tags = jnp.zeros((total, LANES), jnp.float32)
    for r in range(MOST):
        sel = jnp.where(rank == float(r), named_at, 0.0)
        sel_bf = sel.astype(jnp.bfloat16)
        sel_ref[r] = sel_bf
        picked = nn_dot(sel_bf, normed)
        for s in range(segs):
            stage[pl.ds(segs * r + s, total, stride=rows), :] = picked[
                :, LANES * s : LANES * (s + 1)
            ]
        col = jnp.sum(sel * own_label, axis=1, keepdims=True)
        high = jnp.floor(col * (1.0 / 32.0))
        low = col - 32.0 * high
        tags = jnp.where(lane == 2 * r, high, tags)
        tags = jnp.where(lane == 2 * r + 1, low, tags)
    stage[pl.ds(MOST * segs, total, stride=rows), :] = tags
    stage[pl.ds(MOST * segs + 1, total, stride=rows), :] = jnp.zeros_like(tags)
    pay_ref[...] = stage[...].astype(jnp.bfloat16)


def centers_kernel(centers_ref, normed_ref):
    c = centers_ref[...].astype(jnp.float32)
    length = jnp.sqrt(jnp.sum(c * c, axis=1, keepdims=True) + EPSILON)
    normed_ref[...] = (c / length).astype(jnp.bfloat16)


def scores_kernel(pay_ref, normed_ref, rows_ref, cols_ref, exps_ref, stats_ref, stage):
    width = normed_ref.shape[1]
    count = normed_ref.shape[0]
    segs = width // LANES
    rows = MOST * segs + 2
    total = pay_ref.shape[0] // rows
    stage[...] = pay_ref[...].astype(jnp.float32)
    tags = stage[pl.ds(MOST * segs, total, stride=rows), :]
    lane = lax.broadcasted_iota(jnp.int32, (total, LANES), 1)
    stats = jnp.zeros((total, LANES), jnp.float32)
    normed = normed_ref[...]
    for r in range(MOST):
        part = jnp.concatenate(
            [stage[pl.ds(segs * r + s, total, stride=rows), :] for s in range(segs)], axis=1
        ).astype(jnp.bfloat16)
        rows_ref[r] = part
        col = (32.0 * tags[:, 2 * r : 2 * r + 1] + tags[:, 2 * r + 1 : 2 * r + 2] - 1.0).astype(
            jnp.int32
        )
        cols_ref[r] = jnp.broadcast_to(col, (total, LANES))
        scores = LOGIT_SCALE * nt_dot(part, normed)
        hit = lax.broadcasted_iota(jnp.int32, (total, count), 1) == col
        scores = jnp.where(hit, scores - LOGIT_SCALE * MARGIN, scores)
        exps = jnp.exp(scores)
        exps_ref[r] = exps
        stats = jnp.where(lane == r, jnp.sum(exps, axis=1, keepdims=True), stats)
        target = jnp.sum(jnp.where(hit, scores, 0.0), axis=1, keepdims=True)
        stats = jnp.where(lane == MOST + r, target, stats)
    stats_ref[...] = stats


def partial_kernel(exps_ref, cols_ref, normed_ref, sums_ref, hits_ref):
    total, count = exps_ref.shape[1:]
    normed = normed_ref[...]
    for r in range(MOST):
        hit = lax.broadcasted_iota(jnp.int32, (total, count), 1) == cols_ref[r][:, 0:1]
        sums_ref[r] = LOGIT_SCALE * nn_dot(exps_ref[r].astype(jnp.bfloat16), normed)
        hits_ref[r] = LOGIT_SCALE * nn_dot(hit.astype(jnp.float32).astype(jnp.bfloat16), normed)


def totals_kernel(stats_ref, sel_ref, gain_ref, back_ref, loss_ref):
    total = stats_ref.shape[0]
    stats = stats_ref[...]
    gain = gain_ref[...].astype(jnp.float32)
    sels = [sel_ref[r].astype(jnp.float32) for r in range(MOST)]
    denom = 0.0
    target = 0.0
    for r in range(MOST):
        denom = denom + jnp.sum(sels[r] * stats[:, r : r + 1], axis=0, keepdims=True)
        target = target + jnp.sum(
            sels[r] * stats[:, MOST + r : MOST + r + 1], axis=0, keepdims=True
        )
    loss_ref[...] = jnp.log(denom) - target
    factor = gain / denom
    lane = lax.broadcasted_iota(jnp.int32, (total, LANES), 1)
    back = jnp.zeros((total, LANES), jnp.float32)
    for r in range(MOST):
        back = jnp.where(lane == r, jnp.sum(sels[r] * factor, axis=1, keepdims=True), back)
        back = jnp.where(lane == MOST + r, jnp.sum(sels[r] * gain, axis=1, keepdims=True), back)
    back_ref[...] = back


def return_kernel(fac_ref, sums_ref, hits_ref, out_ref, stage):
    total = fac_ref.shape[0]
    width = sums_ref.shape[2]
    segs = width // LANES
    fac = fac_ref[...]
    for r in range(MOST):
        grads = fac[:, r : r + 1] * sums_ref[r] - fac[:, MOST + r : MOST + r + 1] * hits_ref[r]
        for s in range(segs):
            stage[pl.ds(segs * r + s, total, stride=MOST * segs), :] = grads[
                :, LANES * s : LANES * (s + 1)
            ]
    out_ref[...] = stage[...].astype(jnp.bfloat16)


def center_grad_kernel(fac_ref, exps_ref, cols_ref, rows_ref, centers_ref, out_ref):
    total, count = exps_ref.shape[1:]
    fac = fac_ref[...]
    unit_grad = jnp.zeros(out_ref.shape, jnp.float32)
    for r in range(MOST):
        hit = lax.broadcasted_iota(jnp.int32, (total, count), 1) == cols_ref[r][:, 0:1]
        weights = fac[:, r : r + 1] * exps_ref[r] - jnp.where(
            hit, fac[:, MOST + r : MOST + r + 1], 0.0
        )
        unit_grad = unit_grad + tn_dot(weights.astype(jnp.bfloat16), rows_ref[r])
    unit_grad = LOGIT_SCALE * unit_grad
    c = centers_ref[...].astype(jnp.float32)
    length = jnp.sqrt(jnp.sum(c * c, axis=1, keepdims=True) + EPSILON)
    unit = c / length
    along = jnp.sum(unit * unit_grad, axis=1, keepdims=True)
    out_ref[...] = ((unit_grad - unit * along) / length).astype(jnp.bfloat16)


def combine_kernel(back_ref, sel_ref, feat_ref, out_ref, stage):
    samples, width = feat_ref.shape
    total = sel_ref.shape[1]
    segs = width // LANES
    stage[...] = back_ref[...].astype(jnp.float32)
    unit_grad = jnp.zeros((samples, width), jnp.float32)
    for r in range(MOST):
        part = jnp.concatenate(
            [stage[pl.ds(segs * r + s, total, stride=MOST * segs), :] for s in range(segs)],
            axis=1,
        ).astype(jnp.bfloat16)
        unit_grad = unit_grad + tn_dot(sel_ref[r], part)
    x = feat_ref[...].astype(jnp.float32)
    norm = jnp.sqrt(jnp.sum(x * x, axis=1, keepdims=True) + EPSILON)
    unit = x / norm
    along = jnp.sum(unit * unit_grad, axis=1, keepdims=True)
    out_ref[...] = (unit_grad - unit * along) / norm


def exchange(x):
    return lax.all_to_all(x, AXES, split_axis=0, concat_axis=0, tiled=True)


def on_device(features, loss_scale, blocks, label_col, block_slot, centers):
    samples, width = features.shape
    total = block_slot.shape[0]
    count = centers.shape[0]
    segs = width // LANES
    rows = MOST * segs + 2
    bf16, f32 = jnp.bfloat16, jnp.float32
    shape = jax.ShapeDtypeStruct
    payload, sel = call(
        dispatch_kernel,
        (shape((total * rows, LANES), bf16), shape((MOST, total, samples), bf16)),
        [pltpu.VMEM((total * rows, LANES), f32)],
        "dispatch",
    )(features, blocks, label_col.reshape(1, samples), block_slot.reshape(1, total))
    payload_in = exchange(payload.reshape(total, rows // 2, 2, LANES)).reshape(total * rows, LANES)
    normed = call(centers_kernel, shape((count, width), bf16), name="normalize")(centers)
    rows_x, cols, exps, stats = call(
        scores_kernel,
        (
            shape((MOST, total, width), bf16),
            shape((MOST, total, LANES), jnp.int32),
            shape((MOST, total, count), f32),
            shape((total, LANES), f32),
        ),
        [pltpu.VMEM((total * rows, LANES), f32)],
        "scores",
    )(payload_in, normed)
    stats_in = exchange(stats.reshape(total, 1, LANES)).reshape(total, LANES)
    sums, hits = call(
        partial_kernel,
        (shape((MOST, total, width), f32), shape((MOST, total, width), f32)),
        name="partial",
    )(exps, cols, normed)
    factors, loss = call(
        totals_kernel, (shape((total, LANES), f32), shape((1, samples), f32)), name="totals"
    )(stats_in, sel, loss_scale.reshape(1, samples))
    factors_in = exchange(factors.reshape(total, 1, LANES)).reshape(total, LANES)
    returned = call(
        return_kernel,
        shape((total * MOST * segs, LANES), bf16),
        [pltpu.VMEM((total * MOST * segs, LANES), f32)],
        "returned",
    )(factors_in, sums, hits)
    back = exchange(returned.reshape(total, MOST, segs, LANES)).reshape(total * MOST * segs, LANES)
    center_grad = call(center_grad_kernel, shape((count, width), bf16), name="center_grad")(
        factors_in, exps, cols, rows_x, centers
    )
    feature_grad = call(
        combine_kernel,
        shape((samples, width), f32),
        [pltpu.VMEM((total * MOST * segs, LANES), f32)],
        "combine",
    )(back, sel, features)
    return (loss.reshape(samples), feature_grad, center_grad)


def solution(mesh):
    placed = (
        P(AXES, None),
        P(AXES),
        P(AXES, None),
        P(AXES),
        P(),
        P(AXES, None),
    )
    return jax.shard_map(
        on_device,
        mesh=mesh,
        in_specs=placed,
        out_specs=(P(AXES), P(AXES, None), P(AXES, None)),
        check_vma=False,
    )
```

```python
import jax
import jax.numpy as jnp
from jax import lax
from jax.experimental import pallas as pl
from jax.experimental.pallas import tpu as pltpu
from jax.sharding import PartitionSpec as P

BLOCK = 1024
MOST = 3
LANES = 128
MARGIN = 0.35
LOGIT_SCALE = 64.0
EPSILON = 1e-06
AXES = ("dp", "grp")

MIB = 1024 * 1024


def nt_dot(a, b):
    return lax.dot_general(a, b, (((1,), (1,)), ((), ())), preferred_element_type=jnp.float32)


def tn_dot(a, b):
    return lax.dot_general(a, b, (((0,), (0,)), ((), ())), preferred_element_type=jnp.float32)


def nn_dot(a, b):
    return jnp.dot(a, b, preferred_element_type=jnp.float32)


WHOLE = pl.BlockSpec(memory_space=pltpu.VMEM)


def block(shape, place):
    return pl.BlockSpec(shape, place)


def call(name, kernel, args, outs, scratch=(), grid=(), ins=None, to=None, limit=28):
    return pl.pallas_call(
        kernel,
        out_shape=tuple(outs),
        grid=grid,
        in_specs=ins or [WHOLE] * len(args),
        out_specs=to or tuple(WHOLE for _ in outs),
        scratch_shapes=list(scratch),
        compiler_params=pltpu.CompilerParams(vmem_limit_bytes=limit * MIB),
        name=name,
    )(*args)


def near(x):
    return pltpu.with_memory_space_constraint(x, pltpu.VMEM)


def away(x):
    return pltpu.with_memory_space_constraint(x, pltpu.HBM)


def dispatch_kernel(feat_ref, blocks_ref, label_ref, slot_ref, pay_ref, sel_ref, stage):
    samples, width = feat_ref.shape
    total = slot_ref.shape[1]
    segs = width // LANES
    rows = MOST * segs + 2
    x = feat_ref[...].astype(jnp.float32)
    norm = jnp.sqrt(jnp.sum(x * x, axis=1, keepdims=True) + EPSILON)
    normed = (x / norm).astype(jnp.bfloat16)
    named_by = blocks_ref[...]
    block_iota = lax.broadcasted_iota(jnp.int32, (total, samples), 0)
    own = block_iota == named_by[0:1]
    named = own
    for k in range(1, blocks_ref.shape[0]):
        named = named | (block_iota == named_by[k : k + 1])
    both = jnp.concatenate([named.astype(jnp.float32), own.astype(jnp.float32)], axis=1)
    one_hot = (lax.broadcasted_iota(jnp.int32, (total, total), 0) == slot_ref[...]).astype(
        jnp.float32
    ).astype(jnp.bfloat16)
    both_at = nn_dot(one_hot, both.astype(jnp.bfloat16))
    named_at = both_at[:, :samples]
    own_at = both_at[:, samples:]
    before = (
        lax.broadcasted_iota(jnp.int32, (samples, samples), 0)
        < lax.broadcasted_iota(jnp.int32, (samples, samples), 1)
    ).astype(jnp.float32).astype(jnp.bfloat16)
    rank = nn_dot(named_at.astype(jnp.bfloat16), before)
    label = label_ref[...].astype(jnp.float32) + 1.0
    own_label = own_at * label
    lane = lax.broadcasted_iota(jnp.int32, (total, LANES), 1)
    tags = jnp.zeros((total, LANES), jnp.float32)
    for r in range(MOST):
        sel = jnp.where(rank == float(r), named_at, 0.0)
        sel_bf = sel.astype(jnp.bfloat16)
        sel_ref[r] = sel_bf
        picked = nn_dot(sel_bf, normed)
        for s in range(segs):
            stage[pl.ds(segs * r + s, total, stride=rows), :] = picked[
                :, LANES * s : LANES * (s + 1)
            ]
        col = jnp.sum(sel * own_label, axis=1, keepdims=True)
        high = jnp.floor(col * (1.0 / 32.0))
        low = col - 32.0 * high
        tags = jnp.where(lane == 2 * r, high, tags)
        tags = jnp.where(lane == 2 * r + 1, low, tags)
    stage[pl.ds(MOST * segs, total, stride=rows), :] = tags
    stage[pl.ds(MOST * segs + 1, total, stride=rows), :] = jnp.zeros_like(tags)
    pay_ref[...] = stage[...].astype(jnp.bfloat16)


def centers_kernel(centers_ref, scaled_ref, across_ref):
    c = centers_ref[...].astype(jnp.float32)
    length = jnp.sqrt(jnp.sum(c * c, axis=1, keepdims=True) + EPSILON)
    scaled = LOGIT_SCALE * (c / length).astype(jnp.bfloat16).astype(jnp.float32)
    scaled_ref[...] = scaled.astype(jnp.bfloat16)
    across_ref[...] = scaled.T.astype(jnp.bfloat16)


def scores_kernel(pay_ref, across_ref, rows_ref, exps_ref, cols_ref, stats_ref, stage):
    width, count = across_ref.shape
    segs = width // LANES
    rows = MOST * segs + 2
    total = pay_ref.shape[0] // rows
    r = pl.program_id(0)

    @pl.when(r == 0)
    def _():
        stage[...] = pay_ref[...].astype(jnp.float32)
        cols_ref[...] = jnp.zeros_like(cols_ref)
        stats_ref[...] = jnp.zeros_like(stats_ref)

    lane = lax.broadcasted_iota(jnp.int32, (total, LANES), 1)
    tags = stage[pl.ds(MOST * segs, total, stride=rows), :]
    shares = jnp.where(lane == 2 * r, 32.0, 0.0) + jnp.where(lane == 2 * r + 1, 1.0, 0.0)
    col = jnp.sum(tags * shares, axis=1, keepdims=True).astype(jnp.int32) - 1
    part = jnp.concatenate(
        [stage[pl.ds(segs * r + s, total, stride=rows), :] for s in range(segs)], axis=1
    ).astype(jnp.bfloat16)
    rows_ref[0] = part
    scores = nn_dot(part, across_ref[...])
    hit = lax.broadcasted_iota(jnp.int32, (total, count), 1) == col
    scores = jnp.where(hit, scores - LOGIT_SCALE * MARGIN, scores)
    exps = jnp.exp(scores)
    exps_ref[0] = exps
    sums = jnp.sum(exps, axis=1, keepdims=True)
    target = jnp.sum(jnp.where(hit, scores, 0.0), axis=1, keepdims=True)
    stats = jnp.where(lane == r, sums, stats_ref[...])
    stats_ref[...] = jnp.where(lane == MOST + r, target, stats)
    cols_ref[...] = jnp.where(lane == r, col, cols_ref[...])


def partial_kernel(exps_ref, cols_ref, scaled_ref, sums_ref, hits_ref):
    total, count = exps_ref.shape[1:]
    r = pl.program_id(0)
    lane = lax.broadcasted_iota(jnp.int32, (total, LANES), 1)
    col = jnp.sum(jnp.where(lane == r, cols_ref[...], 0), axis=1, keepdims=True)
    hit = lax.broadcasted_iota(jnp.int32, (total, count), 1) == col
    exps = jnp.where(hit, 0.0, exps_ref[0]).astype(jnp.bfloat16)
    sums_ref[0] = nn_dot(exps, scaled_ref[...])
    chosen = jnp.where(hit, 1.0, 0.0).astype(jnp.bfloat16)
    hits_ref[0] = nn_dot(chosen, scaled_ref[...]).astype(jnp.bfloat16)


def totals_kernel(stats_ref, sel_ref, gain_ref, back_ref, loss_ref):
    total = stats_ref.shape[0]
    stats = stats_ref[...]
    gain = gain_ref[...].astype(jnp.float32)
    sels = [sel_ref[r].astype(jnp.float32) for r in range(MOST)]
    denom = 0.0
    target = 0.0
    for r in range(MOST):
        denom = denom + jnp.sum(sels[r] * stats[:, r : r + 1], axis=0, keepdims=True)
        target = target + jnp.sum(
            sels[r] * stats[:, MOST + r : MOST + r + 1], axis=0, keepdims=True
        )
    loss_ref[...] = jnp.log(denom) - target
    factor = gain / denom
    lane = lax.broadcasted_iota(jnp.int32, (total, LANES), 1)
    back = jnp.zeros((total, LANES), jnp.float32)
    for r in range(MOST):
        back = jnp.where(lane == r, jnp.sum(sels[r] * factor, axis=1, keepdims=True), back)
        back = jnp.where(lane == MOST + r, jnp.sum(sels[r] * gain, axis=1, keepdims=True), back)
    back_ref[...] = back


def return_kernel(fac_ref, stats_ref, sums_ref, hits_ref, out_ref, stage):
    some, width = sums_ref.shape[1:]
    segs = width // LANES
    fac = fac_ref[pl.ds(pl.multiple_of(pl.program_id(0) * some, some), some), :]
    stats = stats_ref[...]
    for r in range(MOST):
        factor = fac[:, r : r + 1]
        at_label = factor * jnp.exp(stats[:, MOST + r : MOST + r + 1])
        at_label = at_label - fac[:, MOST + r : MOST + r + 1]
        grads = factor * sums_ref[r] + at_label * hits_ref[r].astype(jnp.float32)
        for s in range(segs):
            stage[pl.ds(segs * r + s, some, stride=MOST * segs), :] = grads[
                :, LANES * s : LANES * (s + 1)
            ]
    out_ref[...] = stage[...].astype(jnp.bfloat16)


def center_grad_kernel(fac_ref, exps_ref, cols_ref, rows_ref, centers_ref, out_ref):
    total, count = exps_ref.shape[1:]
    fac = fac_ref[...]
    cols = cols_ref[...]
    unit_grad = jnp.zeros(out_ref.shape, jnp.float32)
    for r in range(MOST):
        hit = lax.broadcasted_iota(jnp.int32, (total, count), 1) == cols[:, r : r + 1]
        weights = fac[:, r : r + 1] * exps_ref[r] - jnp.where(
            hit, fac[:, MOST + r : MOST + r + 1], 0.0
        )
        unit_grad = unit_grad + tn_dot(weights.astype(jnp.bfloat16), rows_ref[r])
    unit_grad = LOGIT_SCALE * unit_grad
    c = centers_ref[...].astype(jnp.float32)
    length = jnp.sqrt(jnp.sum(c * c, axis=1, keepdims=True) + EPSILON)
    unit = c / length
    along = jnp.sum(unit * unit_grad, axis=1, keepdims=True)
    out_ref[...] = ((unit_grad - unit * along) / length).astype(jnp.bfloat16)


def combine_kernel(back_ref, sel_ref, feat_ref, out_ref, stage):
    samples, width = feat_ref.shape
    total = sel_ref.shape[1]
    segs = width // LANES
    stage[...] = back_ref[...].astype(jnp.float32)
    unit_grad = jnp.zeros((samples, width), jnp.float32)
    for r in range(MOST):
        part = jnp.concatenate(
            [stage[pl.ds(segs * r + s, total, stride=MOST * segs), :] for s in range(segs)],
            axis=1,
        ).astype(jnp.bfloat16)
        unit_grad = unit_grad + tn_dot(sel_ref[r], part)
    x = feat_ref[...].astype(jnp.float32)
    norm = jnp.sqrt(jnp.sum(x * x, axis=1, keepdims=True) + EPSILON)
    unit = x / norm
    along = jnp.sum(unit * unit_grad, axis=1, keepdims=True)
    out_ref[...] = (unit_grad - unit * along) / norm


def exchange(x):
    return lax.all_to_all(x, AXES, split_axis=0, concat_axis=0, tiled=True)


def on_device(features, loss_scale, blocks, label_col, block_slot, centers):
    samples, width = features.shape
    total = block_slot.shape[0]
    count = centers.shape[0]
    segs = width // LANES
    rows = MOST * segs + 2
    back_rows = MOST * segs
    bf16, f32 = jnp.bfloat16, jnp.float32
    far, here = pltpu.HBM, pltpu.VMEM
    chunks = 4
    some = total // chunks
    payload, sel = call(
        "dispatch",
        dispatch_kernel,
        tuple(
            away(x)
            for x in (
                features,
                blocks.T,
                label_col.reshape(1, samples),
                block_slot.reshape(1, total),
            )
        ),
        (far((total * rows, LANES), bf16), far((MOST, total, samples), bf16)),
        [here((total * rows, LANES), f32)],
    )
    payload_in = exchange(payload.reshape(total, rows // 2, 2, LANES)).reshape(total * rows, LANES)
    scaled, across = call(
        "normalize",
        centers_kernel,
        (centers,),
        (far((count, width), bf16), far((width, count), bf16)),
    )
    rows_x, exps, cols, stats = call(
        "scores",
        scores_kernel,
        (near(payload_in), away(across)),
        (
            far((MOST, total, width), bf16),
            far((MOST, total, count), f32),
            far((total, LANES), jnp.int32),
            far((total, LANES), f32),
        ),
        [here((total * rows, LANES), f32)],
        grid=(MOST,),
        to=(
            block((1, total, width), lambda r: (r, 0, 0)),
            block((1, total, count), lambda r: (r, 0, 0)),
            block((total, LANES), lambda r: (0, 0)),
            block((total, LANES), lambda r: (0, 0)),
        ),
    )
    stats_in = exchange(stats.reshape(total, 1, LANES)).reshape(total, LANES)
    sums, hits = call(
        "partial",
        partial_kernel,
        (away(exps), away(cols), away(scaled)),
        (far((MOST, total, width), f32), far((MOST, total, width), bf16)),
        grid=(MOST,),
        ins=[block((1, total, count), lambda r: (r, 0, 0)), WHOLE, WHOLE],
        to=(
            block((1, total, width), lambda r: (r, 0, 0)),
            block((1, total, width), lambda r: (r, 0, 0)),
        ),
    )
    factors, loss = call(
        "totals",
        totals_kernel,
        (near(stats_in), near(sel), loss_scale.reshape(1, samples)),
        (far((total, LANES), f32), far((1, samples), f32)),
    )
    factors_in = exchange(factors.reshape(total, 1, LANES)).reshape(total, LANES)
    (returned,) = call(
        "returned",
        return_kernel,
        (near(factors_in), away(stats), away(sums), away(hits)),
        (far((total * back_rows, LANES), bf16),),
        [here((some * back_rows, LANES), f32)],
        grid=(chunks,),
        ins=[
            WHOLE,
            block((some, LANES), lambda d: (d, 0)),
            block((MOST, some, width), lambda d: (0, d, 0)),
            block((MOST, some, width), lambda d: (0, d, 0)),
        ],
        to=(block((some * back_rows, LANES), lambda d: (d, 0)),),
    )
    back = exchange(returned.reshape(total, MOST, segs, LANES)).reshape(total * back_rows, LANES)
    (center_grad,) = call(
        "center_grad",
        center_grad_kernel,
        (near(factors_in), away(exps), away(cols), away(rows_x), away(centers)),
        (far((count, width), bf16),),
    )
    (feature_grad,) = call(
        "combine",
        combine_kernel,
        (near(back), near(sel), away(features)),
        (far((samples, width), f32),),
        [here((total * back_rows, LANES), f32)],
    )
    return (loss.reshape(samples), feature_grad, center_grad)


def solution(mesh):
    placed = (
        P(AXES, None),
        P(AXES),
        P(AXES, None),
        P(AXES),
        P(),
        P(AXES, None),
    )
    return jax.shard_map(
        on_device,
        mesh=mesh,
        in_specs=placed,
        out_specs=(P(AXES), P(AXES, None), P(AXES, None)),
        check_vma=False,
    )
```

```python
import functools

import jax
import jax.numpy as jnp
from jax import lax
from jax.experimental import pallas as pl
from jax.experimental.pallas import tpu as pltpu
from jax.sharding import Mesh
from jax.sharding import PartitionSpec as P

BLOCK = 1024
MOST = 3
LANES = 128
MARGIN = 0.35
LOGIT_SCALE = 64.0
EPSILON = 1e-06
AXES = ("z", "y", "core", "grp")
PLANE = ("y", "core", "grp")

MIB = 1024 * 1024


def nt_dot(a, b):
    return lax.dot_general(a, b, (((1,), (1,)), ((), ())), preferred_element_type=jnp.float32)


def tn_dot(a, b):
    return lax.dot_general(a, b, (((0,), (0,)), ((), ())), preferred_element_type=jnp.float32)


def nn_dot(a, b):
    return jnp.dot(a, b, preferred_element_type=jnp.float32)


WHOLE = pl.BlockSpec(memory_space=pltpu.VMEM)


def block(shape, place):
    return pl.BlockSpec(shape, place)


def call(name, kernel, args, outs, scratch=(), grid=(), ins=None, to=None, limit=28):
    return pl.pallas_call(
        kernel,
        out_shape=tuple(outs),
        grid=grid,
        in_specs=ins or [WHOLE] * len(args),
        out_specs=to or tuple(WHOLE for _ in outs),
        scratch_shapes=list(scratch),
        compiler_params=pltpu.CompilerParams(vmem_limit_bytes=limit * MIB),
        name=name,
    )(*args)


def near(x):
    return pltpu.with_memory_space_constraint(x, pltpu.VMEM)


def away(x):
    return pltpu.with_memory_space_constraint(x, pltpu.HBM)


def dispatch_kernel(
    feat_ref, blocks_ref, label_ref, gain_ref, slot_ref, pay_ref, sel_ref, stage
):
    samples, width = feat_ref.shape
    total = slot_ref.shape[1]
    segs = width // LANES
    rows = MOST * segs + 2
    x = feat_ref[...].astype(jnp.float32)
    norm = jnp.sqrt(jnp.sum(x * x, axis=1, keepdims=True) + EPSILON)
    normed = (x / norm).astype(jnp.bfloat16)
    named_by = blocks_ref[...]
    block_iota = lax.broadcasted_iota(jnp.int32, (total, samples), 0)
    own = block_iota == named_by[0:1]
    named = own
    for k in range(1, blocks_ref.shape[0]):
        named = named | (block_iota == named_by[k : k + 1])
    both = jnp.concatenate([named.astype(jnp.float32), own.astype(jnp.float32)], axis=1)
    one_hot = (lax.broadcasted_iota(jnp.int32, (total, total), 0) == slot_ref[...]).astype(
        jnp.float32
    ).astype(jnp.bfloat16)
    both_at = nn_dot(one_hot, both.astype(jnp.bfloat16))
    named_at = both_at[:, :samples]
    own_at = both_at[:, samples:]
    before = (
        lax.broadcasted_iota(jnp.int32, (samples, samples), 0)
        < lax.broadcasted_iota(jnp.int32, (samples, samples), 1)
    ).astype(jnp.float32).astype(jnp.bfloat16)
    rank = nn_dot(named_at.astype(jnp.bfloat16), before)
    label = label_ref[...].astype(jnp.float32) + 1.0
    high = jnp.floor(label * (1.0 / 32.0))
    low = label - 32.0 * high
    gain = gain_ref[...].astype(jnp.float32)
    field = lax.broadcasted_iota(jnp.int32, (LANES, samples), 0)
    ids = lax.broadcasted_iota(jnp.int32, (LANES, samples), 1).astype(jnp.float32) + 1.0
    tags = jnp.zeros((total, LANES), jnp.float32)
    for r in range(MOST):
        sel = jnp.where(rank == float(r), named_at, 0.0)
        sel_bf = sel.astype(jnp.bfloat16)
        sel_ref[r] = sel_bf
        picked = nn_dot(sel_bf, normed)
        for s in range(segs):
            stage[pl.ds(segs * r + s, total, stride=rows), :] = picked[
                :, LANES * s : LANES * (s + 1)
            ]
        own_tags = jnp.where(field == 4 * r, high, jnp.where(field == 4 * r + 1, low, 0.0))
        all_tags = jnp.where(field == 4 * r + 2, ids, jnp.where(field == 4 * r + 3, gain, 0.0))
        tags = tags + nt_dot((sel * own_at).astype(jnp.bfloat16), own_tags.astype(jnp.bfloat16))
        tags = tags + nt_dot(sel_bf, all_tags.astype(jnp.bfloat16))
    stage[pl.ds(MOST * segs, total, stride=rows), :] = tags
    stage[pl.ds(MOST * segs + 1, total, stride=rows), :] = jnp.zeros_like(tags)
    pay_ref[...] = stage[...].astype(jnp.bfloat16)


def centers_kernel(centers_ref, scaled_ref, across_ref):
    c = centers_ref[...].astype(jnp.float32)
    length = jnp.sqrt(jnp.sum(c * c, axis=1, keepdims=True) + EPSILON)
    scaled = LOGIT_SCALE * (c / length).astype(jnp.bfloat16).astype(jnp.float32)
    scaled_ref[...] = scaled.astype(jnp.bfloat16)
    across_ref[...] = scaled.T.astype(jnp.bfloat16)


def scores_kernel(pay_ref, across_ref, rows_ref, exps_ref, tags_ref, stats_ref, brief_ref, stage):
    width, count = across_ref.shape
    segs = width // LANES
    rows = MOST * segs + 2
    total = pay_ref.shape[0] // rows
    peers = brief_ref.shape[0]
    span = LANES * peers // total
    r = pl.program_id(0)

    @pl.when(r == 0)
    def _():
        stage[...] = pay_ref[...].astype(jnp.float32)
        tags_ref[...] = stage[pl.ds(MOST * segs, total, stride=rows), :]
        stats_ref[...] = jnp.zeros_like(stats_ref)

    lane = lax.broadcasted_iota(jnp.int32, (total, LANES), 1)
    shares = jnp.where(lane == 4 * r, 32.0, 0.0) + jnp.where(lane == 4 * r + 1, 1.0, 0.0)
    col = jnp.sum(tags_ref[...] * shares, axis=1, keepdims=True).astype(jnp.int32) - 1
    part = jnp.concatenate(
        [stage[pl.ds(segs * r + s, total, stride=rows), :] for s in range(segs)], axis=1
    ).astype(jnp.bfloat16)
    rows_ref[0] = part
    scores = nn_dot(part, across_ref[...])
    hit = lax.broadcasted_iota(jnp.int32, (total, count), 1) == col
    scores = jnp.where(hit, scores - LOGIT_SCALE * MARGIN, scores)
    exps = jnp.exp(scores)
    exps_ref[0] = exps
    sums = jnp.sum(exps, axis=1, keepdims=True)
    target = jnp.sum(jnp.where(hit, scores, 0.0), axis=1, keepdims=True)
    stats = jnp.where(lane == r, sums, stats_ref[...])
    stats_ref[...] = jnp.where(lane == MOST + r, target, stats)

    @pl.when(r == MOST - 1)
    def _():
        stats = stats_ref[...]
        for k in range(MOST):
            ids = tags_ref[:, 4 * k + 2 : 4 * k + 3] - 1.0
            stats = jnp.where(lane == 2 * MOST + k, ids, stats)
        brief = stats[:peers]
        for j in range(1, total // peers):
            brief = brief + pltpu.roll(stats[peers * j : peers * (j + 1)], span * j, 1)
        brief_ref[...] = brief


def partial_kernel(exps_ref, tags_ref, scaled_ref, sums_ref, hits_ref):
    total, count = exps_ref.shape[1:]
    r = pl.program_id(0)
    lane = lax.broadcasted_iota(jnp.int32, (total, LANES), 1)
    shares = jnp.where(lane == 4 * r, 32.0, 0.0) + jnp.where(lane == 4 * r + 1, 1.0, 0.0)
    col = jnp.sum(tags_ref[...] * shares, axis=1, keepdims=True).astype(jnp.int32) - 1
    hit = lax.broadcasted_iota(jnp.int32, (total, count), 1) == col
    exps = jnp.where(hit, 0.0, exps_ref[0]).astype(jnp.bfloat16)
    sums_ref[0] = nn_dot(exps, scaled_ref[...])
    chosen = jnp.where(hit, 1.0, 0.0).astype(jnp.bfloat16)
    hits_ref[0] = nn_dot(chosen, scaled_ref[...]).astype(jnp.bfloat16)


def gather_kernel(brief_ref, out_ref):
    peers = brief_ref.shape[0]
    copies = out_ref.shape[0]
    groups = out_ref.shape[1] // 2
    span = LANES // groups
    brief = brief_ref[...]
    lane = lax.broadcasted_iota(jnp.int32, (peers, LANES), 1).astype(jnp.float32)
    totals, targets = [], []
    for j in range(groups):
        total = jnp.zeros((peers, LANES), jnp.float32)
        target = jnp.zeros((peers, LANES), jnp.float32)
        for r in range(MOST):
            at = span * j + r
            hit = lane == brief[:, at + 2 * MOST : at + 2 * MOST + 1]
            total = total + jnp.where(hit, brief[:, at : at + 1], 0.0)
            target = target + jnp.where(hit, brief[:, at + MOST : at + MOST + 1], 0.0)
        totals.append(jnp.sum(total, axis=0, keepdims=True))
        targets.append(jnp.sum(target, axis=0, keepdims=True))
    dense = jnp.concatenate(totals + targets, axis=0)
    for k in range(copies):
        out_ref[k] = dense


def totals_kernel(dense_ref, brief_ref, back_ref, loss_ref):
    peers = brief_ref.shape[0]
    copies, pairs = dense_ref.shape[:2]
    groups = pairs // 2
    span = LANES // groups
    dense = dense_ref[0]
    for k in range(1, copies):
        dense = dense + dense_ref[k]
    denom = dense[:groups]
    loss_ref[...] = jnp.log(denom) - dense[groups:]
    brief = brief_ref[...]
    lane_int = lax.broadcasted_iota(jnp.int32, (peers, LANES), 1)
    lane = lane_int.astype(jnp.float32)
    back = jnp.zeros((peers, LANES), jnp.float32)
    for j in range(groups):
        for r in range(MOST):
            at = span * j + r
            hit = lane == brief[:, at + 2 * MOST : at + 2 * MOST + 1]
            mine = jnp.sum(jnp.where(hit, denom[j : j + 1], 0.0), axis=1, keepdims=True)
            back = jnp.where(lane_int == at, mine, back)
    back_ref[...] = back


def spread(back, total):
    groups = total // back.shape[0]
    span = LANES // groups
    parts = [back]
    for j in range(1, groups):
        parts.append(pltpu.roll(back, LANES - span * j, 1))
    return jnp.concatenate(parts, axis=0)


def factor_of(denom, gain):
    held = gain > 0.0
    return jnp.where(held, gain / jnp.where(held, denom, 1.0), 0.0)


def return_kernel(back_ref, tags_ref, stats_ref, sums_ref, hits_ref, out_ref, stage, denoms):
    some, width = sums_ref.shape[1:]
    segs = width // LANES
    step = pl.program_id(0)

    @pl.when(step == 0)
    def _():
        denoms[...] = spread(back_ref[...], denoms.shape[0])

    denom = denoms[pl.ds(pl.multiple_of(step * some, some), some), :]
    stats = stats_ref[...]
    tags = tags_ref[...]
    for r in range(MOST):
        gain = tags[:, 4 * r + 3 : 4 * r + 4]
        factor = factor_of(denom[:, r : r + 1], gain)
        at_label = factor * jnp.exp(stats[:, MOST + r : MOST + r + 1]) - gain
        grads = factor * sums_ref[r] + at_label * hits_ref[r].astype(jnp.float32)
        for s in range(segs):
            stage[pl.ds(segs * r + s, some, stride=MOST * segs), :] = grads[
                :, LANES * s : LANES * (s + 1)
            ]
    out_ref[...] = stage[...].astype(jnp.bfloat16)


def center_grad_kernel(back_ref, exps_ref, tags_ref, rows_ref, centers_ref, out_ref):
    total, count = exps_ref.shape[1:]
    denom = spread(back_ref[...], total)
    tags = tags_ref[...]
    unit_grad = jnp.zeros(out_ref.shape, jnp.float32)
    for r in range(MOST):
        gain = tags[:, 4 * r + 3 : 4 * r + 4]
        factor = factor_of(denom[:, r : r + 1], gain)
        col = 32.0 * tags[:, 4 * r : 4 * r + 1] + tags[:, 4 * r + 1 : 4 * r + 2] - 1.0
        hit = lax.broadcasted_iota(jnp.int32, (total, count), 1) == col.astype(jnp.int32)
        weights = factor * exps_ref[r] - jnp.where(hit, gain, 0.0)
        unit_grad = unit_grad + tn_dot(weights.astype(jnp.bfloat16), rows_ref[r])
    unit_grad = LOGIT_SCALE * unit_grad
    c = centers_ref[...].astype(jnp.float32)
    length = jnp.sqrt(jnp.sum(c * c, axis=1, keepdims=True) + EPSILON)
    unit = c / length
    along = jnp.sum(unit * unit_grad, axis=1, keepdims=True)
    out_ref[...] = ((unit_grad - unit * along) / length).astype(jnp.bfloat16)


def combine_kernel(back_ref, sel_ref, feat_ref, out_ref, stage):
    samples, width = feat_ref.shape
    total = sel_ref.shape[1]
    segs = width // LANES
    stage[...] = back_ref[...].astype(jnp.float32)
    unit_grad = jnp.zeros((samples, width), jnp.float32)
    for r in range(MOST):
        part = jnp.concatenate(
            [stage[pl.ds(segs * r + s, total, stride=MOST * segs), :] for s in range(segs)],
            axis=1,
        ).astype(jnp.bfloat16)
        unit_grad = unit_grad + tn_dot(sel_ref[r], part)
    x = feat_ref[...].astype(jnp.float32)
    norm = jnp.sqrt(jnp.sum(x * x, axis=1, keepdims=True) + EPSILON)
    unit = x / norm
    along = jnp.sum(unit * unit_grad, axis=1, keepdims=True)
    out_ref[...] = (unit_grad - unit * along) / norm


def exchange(x, axes=AXES):
    return lax.all_to_all(x, axes, split_axis=0, concat_axis=0, tiled=True)


def place():
    return lax.axis_index("z")


def on_device(groups, features, loss_scale, blocks, label_col, block_slot, centers):
    samples, width = features.shape
    total = block_slot.shape[0]
    count = centers.shape[0]
    segs = width // LANES
    rows = MOST * segs + 2
    back_rows = MOST * segs
    bf16, f32 = jnp.bfloat16, jnp.float32
    far, here = pltpu.HBM, pltpu.VMEM
    chunks = 4
    some = total // chunks
    payload, sel = call(
        "dispatch",
        dispatch_kernel,
        tuple(
            away(x)
            for x in (
                features,
                blocks.T,
                label_col.reshape(1, samples),
                loss_scale.reshape(1, samples),
                block_slot.reshape(1, total),
            )
        ),
        (far((total * rows, LANES), bf16), far((MOST, total, samples), bf16)),
        [here((total * rows, LANES), f32)],
    )
    payload_in = exchange(payload.reshape(total, rows // 2, 2, LANES)).reshape(total * rows, LANES)
    scaled, across = call(
        "normalize",
        centers_kernel,
        (centers,),
        (far((count, width), bf16), far((width, count), bf16)),
    )
    peers = total // groups
    rows_x, exps, tags, stats, brief = call(
        "scores",
        scores_kernel,
        (near(payload_in), away(across)),
        (
            far((MOST, total, width), bf16),
            far((MOST, total, count), f32),
            far((total, LANES), f32),
            far((total, LANES), f32),
            far((peers, LANES), f32),
        ),
        [here((total * rows, LANES), f32)],
        grid=(MOST,),
        to=(
            block((1, total, width), lambda r: (r, 0, 0)),
            block((1, total, count), lambda r: (r, 0, 0)),
            block((total, LANES), lambda r: (0, 0)),
            block((total, LANES), lambda r: (0, 0)),
            block((peers, LANES), lambda r: (0, 0)),
        ),
    )
    brief_in = exchange(brief.reshape(peers, 1, LANES), PLANE).reshape(peers, LANES)
    (dense,) = call(
        "gather", gather_kernel, (near(brief_in),), (far((groups, 2 * groups, LANES), f32),)
    )
    dense_in = exchange(dense, ("z",))
    denoms, losses = call(
        "totals",
        totals_kernel,
        (near(dense_in), near(brief_in)),
        (far((peers, LANES), f32), far((groups, LANES), f32)),
    )
    denoms_in = exchange(denoms.reshape(peers, 1, LANES), PLANE).reshape(peers, LANES)
    loss = lax.dynamic_index_in_dim(losses, place(), 0, keepdims=False)
    sums, hits = call(
        "partial",
        partial_kernel,
        (away(exps), away(tags), away(scaled)),
        (far((MOST, total, width), f32), far((MOST, total, width), bf16)),
        grid=(MOST,),
        ins=[block((1, total, count), lambda r: (r, 0, 0)), WHOLE, WHOLE],
        to=(
            block((1, total, width), lambda r: (r, 0, 0)),
            block((1, total, width), lambda r: (r, 0, 0)),
        ),
    )
    (returned,) = call(
        "returned",
        return_kernel,
        (near(denoms_in), away(tags), away(stats), away(sums), away(hits)),
        (far((total * back_rows, LANES), bf16),),
        [here((some * back_rows, LANES), f32), here((total, LANES), f32)],
        grid=(chunks,),
        ins=[
            WHOLE,
            block((some, LANES), lambda d: (d, 0)),
            block((some, LANES), lambda d: (d, 0)),
            block((MOST, some, width), lambda d: (0, d, 0)),
            block((MOST, some, width), lambda d: (0, d, 0)),
        ],
        to=(block((some * back_rows, LANES), lambda d: (d, 0)),),
    )
    back = exchange(returned.reshape(total, MOST, segs, LANES)).reshape(total * back_rows, LANES)
    (center_grad,) = call(
        "center_grad",
        center_grad_kernel,
        (near(denoms_in), away(exps), away(tags), away(rows_x), away(centers)),
        (far((count, width), bf16),),
    )
    (feature_grad,) = call(
        "combine",
        combine_kernel,
        (near(back), near(sel), away(features)),
        (far((samples, width), f32),),
        [here((total * back_rows, LANES), f32)],
    )
    return (loss, feature_grad, center_grad)


def solution(mesh):
    groups = 8
    split = (groups, mesh.shape["dp"] // groups // 2, 2, mesh.shape["grp"])
    mesh = Mesh(mesh.devices.reshape(split), AXES)
    placed = (
        P(AXES, None),
        P(AXES),
        P(AXES, None),
        P(AXES),
        P(),
        P(AXES, None),
    )
    return jax.shard_map(
        functools.partial(on_device, groups),
        mesh=mesh,
        in_specs=placed,
        out_specs=(P(AXES), P(AXES, None), P(AXES, None)),
        check_vma=False,
    )
```

```python
import functools

import jax
import jax.numpy as jnp
from jax import lax
from jax.experimental import pallas as pl
from jax.experimental.pallas import tpu as pltpu
from jax.sharding import Mesh
from jax.sharding import PartitionSpec as P

BLOCK = 1024
MOST = 3
LANES = 128
MARGIN = 0.35
LOGIT_SCALE = 64.0
EPSILON = 1e-06
AXES = ("z", "y", "core", "grp")
PLANE = ("y", "core", "grp")

MIB = 1024 * 1024


def nt_dot(a, b):
    return lax.dot_general(a, b, (((1,), (1,)), ((), ())), preferred_element_type=jnp.float32)


def tn_dot(a, b):
    return lax.dot_general(a, b, (((0,), (0,)), ((), ())), preferred_element_type=jnp.float32)


def nn_dot(a, b):
    return jnp.dot(a, b, preferred_element_type=jnp.float32)


WHOLE = pl.BlockSpec(memory_space=pltpu.VMEM)


AWAY = pl.BlockSpec(memory_space=pl.ANY)


def block(shape, place):
    return pl.BlockSpec(shape, place)


def call(name, kernel, args, outs, scratch=(), grid=(), ins=None, to=None, limit=28):
    return pl.pallas_call(
        kernel,
        out_shape=tuple(outs),
        grid=grid,
        in_specs=ins or [WHOLE] * len(args),
        out_specs=to or tuple(WHOLE for _ in outs),
        scratch_shapes=list(scratch),
        compiler_params=pltpu.CompilerParams(vmem_limit_bytes=limit * MIB),
        name=name,
    )(*args)


def near(x):
    return pltpu.with_memory_space_constraint(x, pltpu.VMEM)


def away(x):
    return pltpu.with_memory_space_constraint(x, pltpu.HBM)


def dispatch_kernel(
    feat_ref, blocks_ref, label_ref, gain_ref, slot_ref, pay_ref, sel_ref, stage, packed, sems
):
    samples, width = feat_ref.shape
    total = slot_ref.shape[1]
    segs = width // LANES
    rows = MOST * segs + 2
    x = feat_ref[...].astype(jnp.float32)
    norm = jnp.sqrt(jnp.sum(x * x, axis=1, keepdims=True) + EPSILON)
    normed = (x / norm).astype(jnp.bfloat16)
    named_by = blocks_ref[...]
    block_iota = lax.broadcasted_iota(jnp.int32, (total, samples), 0)
    own = block_iota == named_by[0:1]
    named = own
    for k in range(1, blocks_ref.shape[0]):
        named = named | (block_iota == named_by[k : k + 1])
    both = jnp.concatenate([named.astype(jnp.float32), own.astype(jnp.float32)], axis=1)
    one_hot = (lax.broadcasted_iota(jnp.int32, (total, total), 0) == slot_ref[...]).astype(
        jnp.float32
    ).astype(jnp.bfloat16)
    both_at = nn_dot(one_hot, both.astype(jnp.bfloat16))
    named_at = both_at[:, :samples]
    own_at = both_at[:, samples:]
    before = (
        lax.broadcasted_iota(jnp.int32, (samples, samples), 0)
        < lax.broadcasted_iota(jnp.int32, (samples, samples), 1)
    ).astype(jnp.float32).astype(jnp.bfloat16)
    rank = nn_dot(named_at.astype(jnp.bfloat16), before)
    label = label_ref[...].astype(jnp.float32) + 1.0
    high = jnp.floor(label * (1.0 / 32.0))
    low = label - 32.0 * high
    gain = gain_ref[...].astype(jnp.float32)
    field = lax.broadcasted_iota(jnp.int32, (LANES, samples), 0)
    ids = lax.broadcasted_iota(jnp.int32, (LANES, samples), 1).astype(jnp.float32) + 1.0
    tags = jnp.zeros((total, LANES), jnp.float32)
    sels = []
    for r in range(MOST):
        sel = jnp.where(rank == float(r), named_at, 0.0)
        sels.append(sel.astype(jnp.bfloat16))
        sel_ref[r] = sels[r]
        own_tags = jnp.where(field == 4 * r, high, jnp.where(field == 4 * r + 1, low, 0.0))
        all_tags = jnp.where(field == 4 * r + 2, ids, jnp.where(field == 4 * r + 3, gain, 0.0))
        tags = tags + nt_dot((sel * own_at).astype(jnp.bfloat16), own_tags.astype(jnp.bfloat16))
        tags = tags + nt_dot(sels[r], all_tags.astype(jnp.bfloat16))
    chunks = sems.shape[0]
    some = total // chunks
    copies = []
    for d in range(chunks):
        for r in range(MOST):
            picked = nn_dot(sels[r][some * d : some * (d + 1)], normed)
            for s in range(segs):
                stage[pl.ds(some * rows * d + segs * r + s, some, stride=rows), :] = picked[
                    :, LANES * s : LANES * (s + 1)
                ]
        last = some * rows * d + MOST * segs
        stage[pl.ds(last, some, stride=rows), :] = tags[some * d : some * (d + 1)]
        stage[pl.ds(last + 1, some, stride=rows), :] = jnp.zeros((some, LANES), jnp.float32)
        part = pl.ds(some * rows * d, some * rows)
        packed[part, :] = stage[part, :].astype(jnp.bfloat16)
        copies.append(pltpu.make_async_copy(packed.at[part], pay_ref.at[part], sems.at[d]))
        copies[d].start()
    for copy in copies:
        copy.wait()


def centers_kernel(centers_ref, scaled_ref, across_ref):
    c = centers_ref[...].astype(jnp.float32)
    length = jnp.sqrt(jnp.sum(c * c, axis=1, keepdims=True) + EPSILON)
    scaled = LOGIT_SCALE * (c / length).astype(jnp.bfloat16).astype(jnp.float32)
    scaled_ref[...] = scaled.astype(jnp.bfloat16)
    across_ref[...] = scaled.T.astype(jnp.bfloat16)


def scores_kernel(
    pay_ref, far_ref, rows_ref, exps_ref, tags_ref, stats_ref, brief_ref, stage, across_ref, sem
):
    width, count = across_ref.shape
    segs = width // LANES
    rows = MOST * segs + 2
    total = pay_ref.shape[0] // rows
    peers = brief_ref.shape[0]
    span = LANES * peers // total
    r = pl.program_id(0)

    @pl.when(r == 0)
    def _():
        copy = pltpu.make_async_copy(far_ref, across_ref, sem)
        copy.start()
        stage[...] = pay_ref[...].astype(jnp.float32)
        tags_ref[...] = stage[pl.ds(MOST * segs, total, stride=rows), :]
        stats_ref[...] = jnp.zeros_like(stats_ref)
        copy.wait()

    lane = lax.broadcasted_iota(jnp.int32, (total, LANES), 1)
    shares = jnp.where(lane == 4 * r, 32.0, 0.0) + jnp.where(lane == 4 * r + 1, 1.0, 0.0)
    col = jnp.sum(tags_ref[...] * shares, axis=1, keepdims=True).astype(jnp.int32) - 1
    part = jnp.concatenate(
        [stage[pl.ds(segs * r + s, total, stride=rows), :] for s in range(segs)], axis=1
    ).astype(jnp.bfloat16)
    rows_ref[0] = part
    sums = jnp.zeros((total, LANES), jnp.float32)
    target = jnp.zeros((total, LANES), jnp.float32)
    wide = 2 * LANES
    for c in range(0, count, wide):
        scores = nn_dot(part, across_ref[:, c : c + wide])
        hit = lax.broadcasted_iota(jnp.int32, (total, wide), 1) == col - c
        scores = jnp.where(hit, scores - LOGIT_SCALE * MARGIN, scores)
        exps = jnp.exp(scores)
        exps_ref[0, :, c : c + wide] = exps.astype(jnp.bfloat16)
        at_hit = jnp.where(hit, scores, 0.0)
        for h in range(0, wide, LANES):
            sums = sums + exps[:, h : h + LANES]
            target = target + at_hit[:, h : h + LANES]
    sums = jnp.sum(sums, axis=1, keepdims=True)
    target = jnp.sum(target, axis=1, keepdims=True)
    stats = jnp.where(lane == r, sums, stats_ref[...])
    stats_ref[...] = jnp.where(lane == MOST + r, target, stats)

    @pl.when(r == MOST - 1)
    def _():
        stats = stats_ref[...]
        for k in range(MOST):
            ids = tags_ref[:, 4 * k + 2 : 4 * k + 3] - 1.0
            stats = jnp.where(lane == 2 * MOST + k, ids, stats)
        brief = stats[:peers]
        for j in range(1, total // peers):
            brief = brief + pltpu.roll(stats[peers * j : peers * (j + 1)], span * j, 1)
        brief_ref[...] = brief


def partial_kernel(exps_ref, tags_ref, scaled_ref, sums_ref, hits_ref):
    total, count = exps_ref.shape[1:]
    r = pl.program_id(0)
    lane = lax.broadcasted_iota(jnp.int32, (total, LANES), 1)
    shares = jnp.where(lane == 4 * r, 32.0, 0.0) + jnp.where(lane == 4 * r + 1, 1.0, 0.0)
    col = jnp.sum(tags_ref[...] * shares, axis=1, keepdims=True).astype(jnp.int32) - 1
    hit = lax.broadcasted_iota(jnp.int32, (total, count), 1) == col
    exps = jnp.where(hit, 0.0, exps_ref[0].astype(jnp.float32)).astype(jnp.bfloat16)
    sums_ref[r] = nn_dot(exps, scaled_ref[...]).astype(jnp.bfloat16)
    chosen = jnp.where(hit, 1.0, 0.0).astype(jnp.bfloat16)
    hits_ref[r] = nn_dot(chosen, scaled_ref[...]).astype(jnp.bfloat16)


def gather_kernel(brief_ref, out_ref):
    peers = brief_ref.shape[0]
    copies = out_ref.shape[0]
    groups = out_ref.shape[1] // 2
    span = LANES // groups
    fields = brief_ref[...].T
    ids = lax.broadcasted_iota(jnp.int32, (LANES, peers), 0).astype(jnp.float32)
    field = lax.broadcasted_iota(jnp.int32, (LANES, LANES), 1)
    dense = jnp.zeros((LANES, LANES), jnp.float32)
    for j in range(groups):
        total = jnp.zeros((LANES, peers), jnp.float32)
        target = jnp.zeros((LANES, peers), jnp.float32)
        for r in range(MOST):
            at = span * j + r
            hit = ids == fields[at + 2 * MOST : at + 2 * MOST + 1]
            total = total + jnp.where(hit, fields[at : at + 1], 0.0)
            target = target + jnp.where(hit, fields[at + MOST : at + MOST + 1], 0.0)
        dense = jnp.where(field == j, jnp.sum(total, axis=1, keepdims=True), dense)
        dense = jnp.where(field == groups + j, jnp.sum(target, axis=1, keepdims=True), dense)
    dense = dense.T[: 2 * groups]
    for k in range(copies):
        out_ref[k] = dense


def totals_kernel(dense_ref, brief_ref, back_ref, loss_ref):
    peers = brief_ref.shape[0]
    copies, pairs = dense_ref.shape[:2]
    groups = pairs // 2
    span = LANES // groups
    dense = dense_ref[0]
    for k in range(1, copies):
        dense = dense + dense_ref[k]
    denom = dense[:groups]
    loss_ref[...] = jnp.log(denom) - dense[groups:]
    lane = lax.broadcasted_iota(jnp.int32, (peers, LANES), 1)
    ids = pltpu.roll(brief_ref[...], LANES - 2 * MOST, 1)
    ids = jnp.clip(ids, 0.0, LANES - 1.0).astype(jnp.int32)
    back = jnp.zeros((peers, LANES), jnp.float32)
    for j in range(groups):
        row = jnp.broadcast_to(denom[j : j + 1], (peers, LANES))
        found = jnp.take_along_axis(row, ids, axis=1, mode="promise_in_bounds")
        back = jnp.where(lane // span == j, found, back)
    back_ref[...] = back


def spread(back, total):
    groups = total // back.shape[0]
    span = LANES // groups
    parts = [back]
    for j in range(1, groups):
        parts.append(pltpu.roll(back, LANES - span * j, 1))
    return jnp.concatenate(parts, axis=0)


def factor_of(denom, gain):
    held = gain > 0.0
    return jnp.where(held, gain / jnp.where(held, denom, 1.0), 0.0)


def return_kernel(back_ref, tags_ref, stats_ref, sums_ref, hits_ref, out_ref, stage, denoms):
    some = stats_ref.shape[0]
    width = sums_ref.shape[2]
    segs = width // LANES
    step = pl.program_id(0)
    mine = pl.ds(pl.multiple_of(step * some, some), some)

    @pl.when(step == 0)
    def _():
        denoms[...] = spread(back_ref[...], denoms.shape[0])

    denom = denoms[mine, :]
    stats = stats_ref[...]
    tags = tags_ref[...]
    for r in range(MOST):
        gain = tags[:, 4 * r + 3 : 4 * r + 4]
        factor = factor_of(denom[:, r : r + 1], gain)
        at_label = factor * jnp.exp(stats[:, MOST + r : MOST + r + 1]) - gain
        grads = factor * sums_ref[r, mine, :].astype(jnp.float32)
        grads = grads + at_label * hits_ref[r, mine, :].astype(jnp.float32)
        for s in range(segs):
            stage[pl.ds(segs * r + s, some, stride=MOST * segs), :] = grads[
                :, LANES * s : LANES * (s + 1)
            ]
    out_ref[...] = stage[...].astype(jnp.bfloat16)


def center_grad_kernel(back_ref, exps_ref, tags_ref, stats_ref, rows_ref, centers_ref, out_ref):
    total, count = exps_ref.shape[1:]
    denom = spread(back_ref[...], total)
    tags = tags_ref[...]
    unit_grad = jnp.zeros(out_ref.shape, jnp.float32)
    for r in range(MOST):
        gain = tags[:, 4 * r + 3 : 4 * r + 4]
        factor = factor_of(denom[:, r : r + 1], gain)
        col = 32.0 * tags[:, 4 * r : 4 * r + 1] + tags[:, 4 * r + 1 : 4 * r + 2] - 1.0
        hit = lax.broadcasted_iota(jnp.int32, (total, count), 1) == col.astype(jnp.int32)
        at_label = factor * jnp.exp(stats_ref[:, MOST + r : MOST + r + 1]) - gain
        weights = jnp.where(hit, at_label, factor * exps_ref[r].astype(jnp.float32))
        unit_grad = unit_grad + tn_dot(weights.astype(jnp.bfloat16), rows_ref[r])
    unit_grad = LOGIT_SCALE * unit_grad
    c = centers_ref[...].astype(jnp.float32)
    length = jnp.sqrt(jnp.sum(c * c, axis=1, keepdims=True) + EPSILON)
    unit = c / length
    along = jnp.sum(unit * unit_grad, axis=1, keepdims=True)
    out_ref[...] = ((unit_grad - unit * along) / length).astype(jnp.bfloat16)


def combine_kernel(back_ref, sel_ref, far_ref, out_ref, stage, feat_ref, sem):
    samples, width = feat_ref.shape
    copy = pltpu.make_async_copy(far_ref, feat_ref, sem)
    copy.start()
    total = sel_ref.shape[1]
    segs = width // LANES
    stage[...] = back_ref[...].astype(jnp.float32)
    unit_grad = jnp.zeros((samples, width), jnp.float32)
    for r in range(MOST):
        part = jnp.concatenate(
            [stage[pl.ds(segs * r + s, total, stride=MOST * segs), :] for s in range(segs)],
            axis=1,
        ).astype(jnp.bfloat16)
        unit_grad = unit_grad + tn_dot(sel_ref[r], part)
    copy.wait()
    x = feat_ref[...].astype(jnp.float32)
    norm = jnp.sqrt(jnp.sum(x * x, axis=1, keepdims=True) + EPSILON)
    unit = x / norm
    along = jnp.sum(unit * unit_grad, axis=1, keepdims=True)
    out_ref[...] = (unit_grad - unit * along) / norm


def exchange(x, axes=AXES):
    return lax.all_to_all(x, axes, split_axis=0, concat_axis=0, tiled=True)


def place():
    return lax.axis_index("z")


def on_device(groups, features, loss_scale, blocks, label_col, block_slot, centers):
    samples, width = features.shape
    total = block_slot.shape[0]
    count = centers.shape[0]
    segs = width // LANES
    rows = MOST * segs + 2
    back_rows = MOST * segs
    bf16, f32 = jnp.bfloat16, jnp.float32
    far, here = pltpu.HBM, pltpu.VMEM
    chunks = 4
    some = total // chunks
    payload, sel = call(
        "dispatch",
        dispatch_kernel,
        tuple(
            away(x)
            for x in (
                features,
                blocks.T,
                label_col.reshape(1, samples),
                loss_scale.reshape(1, samples),
                block_slot.reshape(1, total),
            )
        ),
        (far((total * rows, LANES), bf16), far((MOST, total, samples), bf16)),
        [
            here((total * rows, LANES), f32),
            here((total * rows, LANES), bf16),
            pltpu.SemaphoreType.DMA((chunks,)),
        ],
        to=(AWAY, WHOLE),
    )
    payload_in = exchange(payload.reshape(total, rows // 2, 2, LANES)).reshape(total * rows, LANES)
    scaled, across = call(
        "normalize",
        centers_kernel,
        (centers,),
        (far((count, width), bf16), far((width, count), bf16)),
    )
    peers = total // groups
    rows_x, exps, tags, stats, brief = call(
        "scores",
        scores_kernel,
        (near(payload_in), away(across)),
        (
            far((MOST, total, width), bf16),
            far((MOST, total, count), bf16),
            far((total, LANES), f32),
            far((total, LANES), f32),
            far((peers, LANES), f32),
        ),
        [
            here((total * rows, LANES), f32),
            here((width, count), bf16),
            pltpu.SemaphoreType.DMA,
        ],
        grid=(MOST,),
        ins=[WHOLE, AWAY],
        to=(
            block((1, total, width), lambda r: (r, 0, 0)),
            block((1, total, count), lambda r: (r, 0, 0)),
            block((total, LANES), lambda r: (0, 0)),
            block((total, LANES), lambda r: (0, 0)),
            block((peers, LANES), lambda r: (0, 0)),
        ),
    )
    brief_in = exchange(brief.reshape(peers, 1, LANES), PLANE).reshape(peers, LANES)
    (dense,) = call(
        "gather", gather_kernel, (near(brief_in),), (far((groups, 2 * groups, LANES), f32),)
    )
    dense_in = exchange(dense, ("z",))
    denoms, losses = call(
        "totals",
        totals_kernel,
        (near(dense_in), near(brief_in)),
        (far((peers, LANES), f32), far((groups, LANES), f32)),
    )
    denoms_in = exchange(denoms.reshape(peers, 1, LANES), PLANE).reshape(peers, LANES)
    loss = lax.dynamic_index_in_dim(losses, place(), 0, keepdims=False)
    sums, hits = call(
        "partial",
        partial_kernel,
        (away(exps), away(tags), away(scaled)),
        (here((MOST, total, width), bf16), here((MOST, total, width), bf16)),
        grid=(MOST,),
        ins=[block((1, total, count), lambda r: (r, 0, 0)), WHOLE, WHOLE],
    )
    (returned,) = call(
        "returned",
        return_kernel,
        (near(denoms_in), away(tags), away(stats), near(sums), near(hits)),
        (far((total * back_rows, LANES), bf16),),
        [here((some * back_rows, LANES), f32), here((total, LANES), f32)],
        grid=(chunks,),
        ins=[
            WHOLE,
            block((some, LANES), lambda d: (d, 0)),
            block((some, LANES), lambda d: (d, 0)),
            WHOLE,
            WHOLE,
        ],
        to=(block((some * back_rows, LANES), lambda d: (d, 0)),),
    )
    back = exchange(returned.reshape(total, MOST, segs, LANES)).reshape(total * back_rows, LANES)
    (center_grad,) = call(
        "center_grad",
        center_grad_kernel,
        (near(denoms_in), away(exps), away(tags), away(stats), away(rows_x), away(centers)),
        (far((count, width), bf16),),
    )
    (feature_grad,) = call(
        "combine",
        combine_kernel,
        (near(back), near(sel), away(features)),
        (far((samples, width), f32),),
        [
            here((total * back_rows, LANES), f32),
            here((samples, width), bf16),
            pltpu.SemaphoreType.DMA,
        ],
        ins=[WHOLE, WHOLE, AWAY],
    )
    return (loss, feature_grad, center_grad)


def solution(mesh):
    groups = 8
    split = (groups, mesh.shape["dp"] // groups // 2, 2, mesh.shape["grp"])
    mesh = Mesh(mesh.devices.reshape(split), AXES)
    placed = (
        P(AXES, None),
        P(AXES),
        P(AXES, None),
        P(AXES),
        P(),
        P(AXES, None),
    )
    return jax.shard_map(
        functools.partial(on_device, groups),
        mesh=mesh,
        in_specs=placed,
        out_specs=(P(AXES), P(AXES, None), P(AXES, None)),
        check_vma=False,
    )
```

```python
import functools

import jax
import jax.numpy as jnp
from jax import lax
from jax.experimental import pallas as pl
from jax.experimental.pallas import tpu as pltpu
from jax.sharding import Mesh
from jax.sharding import PartitionSpec as P

BLOCK = 1024
MOST = 3
GAP = 4
LANES = 128
MARGIN = 0.35
LOGIT_SCALE = 64.0
EPSILON = 1e-06
AXES = ("z", "y", "core", "grp")
PLANE = ("y", "core", "grp")

MIB = 1024 * 1024


def nt_dot(a, b):
    return lax.dot_general(a, b, (((1,), (1,)), ((), ())), preferred_element_type=jnp.float32)


def tn_dot(a, b):
    return lax.dot_general(a, b, (((0,), (0,)), ((), ())), preferred_element_type=jnp.float32)


def nn_dot(a, b):
    return jnp.dot(a, b, preferred_element_type=jnp.float32)


WHOLE = pl.BlockSpec(memory_space=pltpu.VMEM)


AWAY = pl.BlockSpec(memory_space=pl.ANY)


def block(shape, place):
    return pl.BlockSpec(shape, place)


def call(name, kernel, args, outs, scratch=(), grid=(), ins=None, to=None, limit=28):
    return pl.pallas_call(
        kernel,
        out_shape=tuple(outs),
        grid=grid,
        in_specs=ins or [WHOLE] * len(args),
        out_specs=to or tuple(WHOLE for _ in outs),
        scratch_shapes=list(scratch),
        compiler_params=pltpu.CompilerParams(vmem_limit_bytes=limit * MIB),
        name=name,
    )(*args)


def near(x):
    return pltpu.with_memory_space_constraint(x, pltpu.VMEM)


def away(x):
    return pltpu.with_memory_space_constraint(x, pltpu.HBM)


def dispatch_kernel(
    feat_ref, blocks_ref, label_ref, gain_ref, slot_ref, pay_ref, sel_ref, stage
):
    samples, width = feat_ref.shape
    total = slot_ref.shape[1]
    segs = width // LANES
    rows = MOST * segs + 2
    x = feat_ref[...].astype(jnp.float32)
    norm = jnp.sqrt(jnp.sum(x * x, axis=1, keepdims=True) + EPSILON)
    normed = (x / norm).astype(jnp.bfloat16)
    named_by = blocks_ref[...]
    block_iota = lax.broadcasted_iota(jnp.int32, (total, samples), 0)
    own = block_iota == named_by[0:1]
    named = own
    for k in range(1, blocks_ref.shape[0]):
        named = named | (block_iota == named_by[k : k + 1])
    both = jnp.concatenate([named.astype(jnp.float32), own.astype(jnp.float32)], axis=1)
    one_hot = (lax.broadcasted_iota(jnp.int32, (total, total), 0) == slot_ref[...]).astype(
        jnp.float32
    ).astype(jnp.bfloat16)
    both_at = nn_dot(one_hot, both.astype(jnp.bfloat16))
    named_at = both_at[:, :samples]
    own_at = both_at[:, samples:]
    before = (
        lax.broadcasted_iota(jnp.int32, (samples, samples), 0)
        < lax.broadcasted_iota(jnp.int32, (samples, samples), 1)
    ).astype(jnp.float32).astype(jnp.bfloat16)
    rank = nn_dot(named_at.astype(jnp.bfloat16), before)
    label = label_ref[...].astype(jnp.float32) + 1.0
    high = jnp.floor(label * (1.0 / 32.0))
    low = label - 32.0 * high
    gain = gain_ref[...].astype(jnp.float32)
    field = lax.broadcasted_iota(jnp.int32, (LANES, samples), 0)
    ids = lax.broadcasted_iota(jnp.int32, (LANES, samples), 1).astype(jnp.float32) + 1.0
    tags = jnp.zeros((total, LANES), jnp.float32)
    for r in range(MOST):
        sel = jnp.where(rank == float(r), named_at, 0.0)
        sel_bf = sel.astype(jnp.bfloat16)
        sel_ref[r] = sel_bf
        picked = nn_dot(sel_bf, normed)
        for s in range(segs):
            stage[pl.ds(segs * r + s, total, stride=rows), :] = picked[
                :, LANES * s : LANES * (s + 1)
            ]
        own_tags = jnp.where(field == r, high, jnp.where(field == GAP + r, low, 0.0))
        all_tags = jnp.where(field == 2 * GAP + r, ids, jnp.where(field == 3 * GAP + r, gain, 0.0))
        tags = tags + nt_dot((sel * own_at).astype(jnp.bfloat16), own_tags.astype(jnp.bfloat16))
        tags = tags + nt_dot(sel_bf, all_tags.astype(jnp.bfloat16))
    stage[pl.ds(MOST * segs, total, stride=rows), :] = tags
    stage[pl.ds(MOST * segs + 1, total, stride=rows), :] = jnp.zeros_like(tags)
    pay_ref[...] = stage[...].astype(jnp.bfloat16)


def centers_kernel(centers_ref, scaled_ref, across_ref):
    c = centers_ref[...].astype(jnp.float32)
    length = jnp.sqrt(jnp.sum(c * c, axis=1, keepdims=True) + EPSILON)
    scaled = LOGIT_SCALE * (c / length).astype(jnp.bfloat16).astype(jnp.float32)
    scaled_ref[...] = scaled.astype(jnp.bfloat16)
    across_ref[...] = scaled.T.astype(jnp.bfloat16)


def scores_kernel(
    pay_ref, far_ref, rows_ref, exps_ref, tags_ref, stats_ref, brief_ref, stage, across_ref, sem
):
    width, count = across_ref.shape
    segs = width // LANES
    rows = MOST * segs + 2
    total = pay_ref.shape[0] // rows
    peers = brief_ref.shape[0]
    span = LANES * peers // total
    r = pl.program_id(0)

    @pl.when(r == 0)
    def _():
        copy = pltpu.make_async_copy(far_ref, across_ref, sem)
        copy.start()
        stage[...] = pay_ref[...].astype(jnp.float32)
        tags_ref[...] = stage[pl.ds(MOST * segs, total, stride=rows), :]
        stats_ref[...] = jnp.zeros_like(stats_ref)
        copy.wait()

    lane = lax.broadcasted_iota(jnp.int32, (total, LANES), 1)
    shares = jnp.where(lane == r, 32.0, 0.0) + jnp.where(lane == GAP + r, 1.0, 0.0)
    col = jnp.sum(tags_ref[...] * shares, axis=1, keepdims=True).astype(jnp.int32) - 1
    part = jnp.concatenate(
        [stage[pl.ds(segs * r + s, total, stride=rows), :] for s in range(segs)], axis=1
    ).astype(jnp.bfloat16)
    rows_ref[0] = part
    col_wide = jnp.broadcast_to(col, (total, LANES))
    sums = jnp.zeros((total, LANES), jnp.float32)
    found = jnp.zeros((total, LANES), jnp.float32)
    first = lax.broadcasted_iota(jnp.int32, (1, LANES), 1)
    wide = 2 * LANES
    for c in range(0, count, wide):
        scores = nn_dot(part, across_ref[:, c : c + wide])
        for h in range(0, wide, LANES):
            tile = scores[:, h : h + LANES]
            hit = col_wide == first + (c + h)
            exps = jnp.where(hit, 0.0, jnp.exp(tile))
            exps_ref[0, :, c + h : c + h + LANES] = exps.astype(jnp.bfloat16)
            sums = sums + exps
            found = jnp.where(hit, tile, found)
    own = col >= 0
    target = jnp.sum(found, axis=1, keepdims=True) - LOGIT_SCALE * MARGIN
    target = jnp.where(own, target, 0.0)
    sums = jnp.sum(sums, axis=1, keepdims=True) + jnp.where(own, jnp.exp(target), 0.0)
    stats = jnp.where(lane == r, sums, stats_ref[...])
    stats_ref[...] = jnp.where(lane == GAP + r, target, stats)

    @pl.when(r == MOST - 1)
    def _():
        is_id = (lane >= 2 * GAP) & (lane < 2 * GAP + MOST)
        stats = jnp.where(is_id, tags_ref[...] - 1.0, stats_ref[...])
        brief = stats[:peers]
        for j in range(1, total // peers):
            brief = brief + pltpu.roll(stats[peers * j : peers * (j + 1)], span * j, 1)
        brief_ref[...] = brief


def partial_kernel(exps_ref, tags_ref, scaled_ref, sums_ref, hits_ref):
    total, count = exps_ref.shape[1:]
    r = pl.program_id(0)
    lane = lax.broadcasted_iota(jnp.int32, (total, LANES), 1)
    shares = jnp.where(lane == r, 32.0, 0.0) + jnp.where(lane == GAP + r, 1.0, 0.0)
    col = jnp.sum(tags_ref[...] * shares, axis=1, keepdims=True).astype(jnp.int32) - 1
    hit = lax.broadcasted_iota(jnp.int32, (1, count), 1) == col
    sums_ref[r] = nn_dot(exps_ref[0], scaled_ref[...]).astype(jnp.bfloat16)
    chosen = jnp.where(hit, 1.0, 0.0).astype(jnp.bfloat16)
    hits_ref[r] = nn_dot(chosen, scaled_ref[...]).astype(jnp.bfloat16)


def gather_kernel(brief_ref, out_ref):
    peers = brief_ref.shape[0]
    copies = out_ref.shape[0]
    groups = out_ref.shape[1] // 2
    span = LANES // groups
    fields = brief_ref[...].T
    ids = lax.broadcasted_iota(jnp.int32, (LANES, peers), 0).astype(jnp.float32)
    field = lax.broadcasted_iota(jnp.int32, (LANES, LANES), 1)
    dense = jnp.zeros((LANES, LANES), jnp.float32)
    for j in range(groups):
        total = jnp.zeros((LANES, peers), jnp.float32)
        target = jnp.zeros((LANES, peers), jnp.float32)
        for r in range(MOST):
            at = span * j + r
            hit = ids == fields[at + 2 * GAP : at + 2 * GAP + 1]
            total = total + jnp.where(hit, fields[at : at + 1], 0.0)
            target = target + jnp.where(hit, fields[at + GAP : at + GAP + 1], 0.0)
        dense = jnp.where(field == j, jnp.sum(total, axis=1, keepdims=True), dense)
        dense = jnp.where(field == groups + j, jnp.sum(target, axis=1, keepdims=True), dense)
    dense = dense.T[: 2 * groups]
    for k in range(copies):
        out_ref[k] = dense


def totals_kernel(dense_ref, brief_ref, back_ref, loss_ref):
    peers = brief_ref.shape[0]
    copies, pairs = dense_ref.shape[:2]
    groups = pairs // 2
    span = LANES // groups
    dense = dense_ref[0]
    for k in range(1, copies):
        dense = dense + dense_ref[k]
    denom = dense[:groups]
    loss_ref[...] = jnp.log(denom) - dense[groups:]
    lane = lax.broadcasted_iota(jnp.int32, (peers, LANES), 1)
    ids = pltpu.roll(brief_ref[...], LANES - 2 * GAP, 1)
    ids = jnp.clip(ids, 0.0, LANES - 1.0).astype(jnp.int32)
    back = jnp.zeros((peers, LANES), jnp.float32)
    for j in range(groups):
        row = jnp.broadcast_to(denom[j : j + 1], (peers, LANES))
        found = jnp.take_along_axis(row, ids, axis=1, mode="promise_in_bounds")
        back = jnp.where(lane // span == j, found, back)
    back_ref[...] = back


def spread(back, total):
    groups = total // back.shape[0]
    span = LANES // groups
    parts = [back]
    for j in range(1, groups):
        parts.append(pltpu.roll(back, LANES - span * j, 1))
    return jnp.concatenate(parts, axis=0)


def slot_terms(denom, tags, stats):
    gain = pltpu.roll(tags, LANES - 3 * GAP, 1)
    target = pltpu.roll(stats, LANES - GAP, 1)
    held = gain > 0.0
    factors = jnp.where(held, gain / jnp.where(held, denom, 1.0), 0.0)
    cols = 32.0 * tags + pltpu.roll(tags, LANES - GAP, 1) - 1.0
    return factors, factors * jnp.exp(target) - gain, cols


def return_kernel(back_ref, tags_ref, stats_ref, sums_ref, hits_ref, out_ref, stage, denoms):
    some = stats_ref.shape[0]
    width = sums_ref.shape[2]
    segs = width // LANES
    step = pl.program_id(0)
    mine = pl.ds(pl.multiple_of(step * some, some), some)

    @pl.when(step == 0)
    def _():
        denoms[...] = spread(back_ref[...], denoms.shape[0])

    factors, at_labels, _ = slot_terms(denoms[mine, :], tags_ref[...], stats_ref[...])
    for r in range(MOST):
        grads = factors[:, r : r + 1] * sums_ref[r, mine, :].astype(jnp.float32)
        grads = grads + at_labels[:, r : r + 1] * hits_ref[r, mine, :].astype(jnp.float32)
        for s in range(segs):
            stage[pl.ds(segs * r + s, some, stride=MOST * segs), :] = grads[
                :, LANES * s : LANES * (s + 1)
            ]
    out_ref[...] = stage[...].astype(jnp.bfloat16)


def center_grad_kernel(back_ref, exps_ref, tags_ref, stats_ref, rows_ref, centers_ref, out_ref):
    total, count = exps_ref.shape[1:]
    denom = spread(back_ref[...], total)
    factors, at_labels, cols = slot_terms(denom, tags_ref[...], stats_ref[...])
    cols = cols.astype(jnp.int32)
    unit_grad = jnp.zeros(out_ref.shape, jnp.float32)
    for r in range(MOST):
        hit = lax.broadcasted_iota(jnp.int32, (1, count), 1) == cols[:, r : r + 1]
        weights = factors[:, r : r + 1] * exps_ref[r].astype(jnp.float32)
        weights = jnp.where(hit, at_labels[:, r : r + 1], weights)
        unit_grad = unit_grad + tn_dot(weights.astype(jnp.bfloat16), rows_ref[r])
    unit_grad = LOGIT_SCALE * unit_grad
    c = centers_ref[...].astype(jnp.float32)
    length = jnp.sqrt(jnp.sum(c * c, axis=1, keepdims=True) + EPSILON)
    unit = c / length
    along = jnp.sum(unit * unit_grad, axis=1, keepdims=True)
    out_ref[...] = ((unit_grad - unit * along) / length).astype(jnp.bfloat16)


def combine_kernel(back_ref, sel_ref, far_ref, out_ref, stage, feat_ref, sem):
    samples, width = feat_ref.shape
    copy = pltpu.make_async_copy(far_ref, feat_ref, sem)
    copy.start()
    total = sel_ref.shape[1]
    segs = width // LANES
    stage[...] = back_ref[...].astype(jnp.float32)
    unit_grad = jnp.zeros((samples, width), jnp.float32)
    for r in range(MOST):
        part = jnp.concatenate(
            [stage[pl.ds(segs * r + s, total, stride=MOST * segs), :] for s in range(segs)],
            axis=1,
        ).astype(jnp.bfloat16)
        unit_grad = unit_grad + tn_dot(sel_ref[r], part)
    copy.wait()
    x = feat_ref[...].astype(jnp.float32)
    norm = jnp.sqrt(jnp.sum(x * x, axis=1, keepdims=True) + EPSILON)
    unit = x / norm
    along = jnp.sum(unit * unit_grad, axis=1, keepdims=True)
    out_ref[...] = (unit_grad - unit * along) / norm


def exchange(x, axes=AXES):
    return lax.all_to_all(x, axes, split_axis=0, concat_axis=0, tiled=True)


def place():
    return lax.axis_index("z")


def on_device(groups, features, loss_scale, blocks, label_col, block_slot, centers):
    samples, width = features.shape
    total = block_slot.shape[0]
    count = centers.shape[0]
    segs = width // LANES
    rows = MOST * segs + 2
    back_rows = MOST * segs
    bf16, f32 = jnp.bfloat16, jnp.float32
    far, here = pltpu.HBM, pltpu.VMEM
    chunks = 4
    some = total // chunks
    payload, sel = call(
        "dispatch",
        dispatch_kernel,
        tuple(
            away(x)
            for x in (
                features,
                blocks.T,
                label_col.reshape(1, samples),
                loss_scale.reshape(1, samples),
                block_slot.reshape(1, total),
            )
        ),
        (far((total * rows, LANES), bf16), far((MOST, total, samples), bf16)),
        [here((total * rows, LANES), f32)],
    )
    payload_in = exchange(payload.reshape(total, rows // 2, 2, LANES)).reshape(total * rows, LANES)
    scaled, across = call(
        "normalize",
        centers_kernel,
        (centers,),
        (far((count, width), bf16), far((width, count), bf16)),
    )
    peers = total // groups
    rows_x, exps, tags, stats, brief = call(
        "scores",
        scores_kernel,
        (near(payload_in), away(across)),
        (
            far((MOST, total, width), bf16),
            far((MOST, total, count), bf16),
            far((total, LANES), f32),
            far((total, LANES), f32),
            far((peers, LANES), f32),
        ),
        [
            here((total * rows, LANES), f32),
            here((width, count), bf16),
            pltpu.SemaphoreType.DMA,
        ],
        grid=(MOST,),
        ins=[WHOLE, AWAY],
        to=(
            block((1, total, width), lambda r: (r, 0, 0)),
            block((1, total, count), lambda r: (r, 0, 0)),
            block((total, LANES), lambda r: (0, 0)),
            block((total, LANES), lambda r: (0, 0)),
            block((peers, LANES), lambda r: (0, 0)),
        ),
    )
    brief_in = exchange(brief.reshape(peers, 1, LANES), PLANE).reshape(peers, LANES)
    (dense,) = call(
        "gather", gather_kernel, (near(brief_in),), (far((groups, 2 * groups, LANES), f32),)
    )
    dense_in = exchange(dense, ("z",))
    denoms, losses = call(
        "totals",
        totals_kernel,
        (near(dense_in), near(brief_in)),
        (far((peers, LANES), f32), far((groups, LANES), f32)),
    )
    denoms_in = exchange(denoms.reshape(peers, 1, LANES), PLANE).reshape(peers, LANES)
    loss = lax.dynamic_index_in_dim(losses, place(), 0, keepdims=False)
    sums, hits = call(
        "partial",
        partial_kernel,
        (away(exps), away(tags), away(scaled)),
        (here((MOST, total, width), bf16), here((MOST, total, width), bf16)),
        grid=(MOST,),
        ins=[block((1, total, count), lambda r: (r, 0, 0)), WHOLE, WHOLE],
    )
    (returned,) = call(
        "returned",
        return_kernel,
        (near(denoms_in), away(tags), away(stats), near(sums), near(hits)),
        (far((total * back_rows, LANES), bf16),),
        [here((some * back_rows, LANES), f32), here((total, LANES), f32)],
        grid=(chunks,),
        ins=[
            WHOLE,
            block((some, LANES), lambda d: (d, 0)),
            block((some, LANES), lambda d: (d, 0)),
            WHOLE,
            WHOLE,
        ],
        to=(block((some * back_rows, LANES), lambda d: (d, 0)),),
    )
    back = exchange(returned.reshape(total, MOST, segs, LANES)).reshape(total * back_rows, LANES)
    (center_grad,) = call(
        "center_grad",
        center_grad_kernel,
        (near(denoms_in), away(exps), away(tags), away(stats), away(rows_x), away(centers)),
        (far((count, width), bf16),),
    )
    (feature_grad,) = call(
        "combine",
        combine_kernel,
        (near(back), near(sel), away(features)),
        (far((samples, width), f32),),
        [
            here((total * back_rows, LANES), f32),
            here((samples, width), bf16),
            pltpu.SemaphoreType.DMA,
        ],
        ins=[WHOLE, WHOLE, AWAY],
    )
    return (loss, feature_grad, center_grad)


def solution(mesh):
    groups = 8
    split = (groups, mesh.shape["dp"] // groups // 2, 2, mesh.shape["grp"])
    mesh = Mesh(mesh.devices.reshape(split), AXES)
    placed = (
        P(AXES, None),
        P(AXES),
        P(AXES, None),
        P(AXES),
        P(),
        P(AXES, None),
    )
    return jax.shard_map(
        functools.partial(on_device, groups),
        mesh=mesh,
        in_specs=placed,
        out_specs=(P(AXES), P(AXES, None), P(AXES, None)),
        check_vma=False,
    )
```

```python
import functools

import jax
import jax.numpy as jnp
from jax import lax
from jax.experimental import pallas as pl
from jax.experimental.pallas import tpu as pltpu
from jax.sharding import Mesh
from jax.sharding import PartitionSpec as P

BLOCK = 1024
MOST = 3
GAP = 4
LANES = 128
MARGIN = 0.35
LOGIT_SCALE = 64.0
EPSILON = 1e-06
AXES = ("z", "y", "core", "grp")
PLANE = ("y", "core", "grp")

MIB = 1024 * 1024


def nt_dot(a, b):
    return lax.dot_general(a, b, (((1,), (1,)), ((), ())), preferred_element_type=jnp.float32)


def tn_dot(a, b):
    return lax.dot_general(a, b, (((0,), (0,)), ((), ())), preferred_element_type=jnp.float32)


def nn_dot(a, b):
    return jnp.dot(a, b, preferred_element_type=jnp.float32)


WHOLE = pl.BlockSpec(memory_space=pltpu.VMEM)


AWAY = pl.BlockSpec(memory_space=pl.ANY)


def block(shape, place):
    return pl.BlockSpec(shape, place)


def call(name, kernel, args, outs, scratch=(), grid=(), ins=None, to=None, limit=28):
    return pl.pallas_call(
        kernel,
        out_shape=tuple(outs),
        grid=grid,
        in_specs=ins or [WHOLE] * len(args),
        out_specs=to or tuple(WHOLE for _ in outs),
        scratch_shapes=list(scratch),
        compiler_params=pltpu.CompilerParams(vmem_limit_bytes=limit * MIB),
        name=name,
    )(*args)


def near(x):
    return pltpu.with_memory_space_constraint(x, pltpu.VMEM)


def away(x):
    return pltpu.with_memory_space_constraint(x, pltpu.HBM)


def dispatch_kernel(
    feat_ref, blocks_ref, label_ref, gain_ref, slot_ref, pay_ref, sel_ref, stage
):
    samples, width = feat_ref.shape
    total = slot_ref.shape[1]
    segs = width // LANES
    rows = MOST * segs + 2
    x = feat_ref[...].astype(jnp.float32)
    norm = jnp.sqrt(jnp.sum(x * x, axis=1, keepdims=True) + EPSILON)
    normed = (x / norm).astype(jnp.bfloat16)
    named_by = blocks_ref[...]
    block_iota = lax.broadcasted_iota(jnp.int32, (total, samples), 0)
    own = block_iota == named_by[0:1]
    named = own
    for k in range(1, blocks_ref.shape[0]):
        named = named | (block_iota == named_by[k : k + 1])
    both = jnp.concatenate([named.astype(jnp.float32), own.astype(jnp.float32)], axis=1)
    one_hot = (lax.broadcasted_iota(jnp.int32, (total, total), 0) == slot_ref[...]).astype(
        jnp.float32
    ).astype(jnp.bfloat16)
    both_at = nn_dot(one_hot, both.astype(jnp.bfloat16))
    named_at = both_at[:, :samples]
    own_at = both_at[:, samples:]
    before = (
        lax.broadcasted_iota(jnp.int32, (samples, samples), 0)
        < lax.broadcasted_iota(jnp.int32, (samples, samples), 1)
    ).astype(jnp.float32).astype(jnp.bfloat16)
    rank = nn_dot(named_at.astype(jnp.bfloat16), before)
    label = label_ref[...].astype(jnp.float32) + 1.0
    high = jnp.floor(label * (1.0 / 32.0))
    low = label - 32.0 * high
    gain = gain_ref[...].astype(jnp.float32)
    field = lax.broadcasted_iota(jnp.int32, (LANES, samples), 0)
    ids = lax.broadcasted_iota(jnp.int32, (LANES, samples), 1).astype(jnp.float32) + 1.0
    tags = jnp.zeros((total, LANES), jnp.float32)
    for r in range(MOST):
        sel = jnp.where(rank == float(r), named_at, 0.0)
        sel_bf = sel.astype(jnp.bfloat16)
        sel_ref[r] = sel_bf
        picked = nn_dot(sel_bf, normed)
        for s in range(segs):
            stage[pl.ds(segs * r + s, total, stride=rows), :] = picked[
                :, LANES * s : LANES * (s + 1)
            ]
        own_tags = jnp.where(field == r, high, jnp.where(field == GAP + r, low, 0.0))
        all_tags = jnp.where(field == 2 * GAP + r, ids, jnp.where(field == 3 * GAP + r, gain, 0.0))
        tags = tags + nt_dot((sel * own_at).astype(jnp.bfloat16), own_tags.astype(jnp.bfloat16))
        tags = tags + nt_dot(sel_bf, all_tags.astype(jnp.bfloat16))
    stage[pl.ds(MOST * segs, total, stride=rows), :] = tags
    stage[pl.ds(MOST * segs + 1, total, stride=rows), :] = jnp.zeros_like(tags)
    pay_ref[...] = stage[...].astype(jnp.bfloat16)


def centers_kernel(centers_ref, scaled_ref, across_ref):
    c = centers_ref[...].astype(jnp.float32)
    length = jnp.sqrt(jnp.sum(c * c, axis=1, keepdims=True) + EPSILON)
    scaled = LOGIT_SCALE * (c / length).astype(jnp.bfloat16).astype(jnp.float32)
    scaled_ref[...] = scaled.astype(jnp.bfloat16)
    across_ref[...] = scaled.T.astype(jnp.bfloat16)


def scores_kernel(
    pay_ref, far_ref, rows_ref, exps_ref, tags_ref, stats_ref, brief_ref, stage, across_ref, sem
):
    width, count = across_ref.shape
    segs = width // LANES
    rows = MOST * segs + 2
    total = pay_ref.shape[0] // rows
    peers = brief_ref.shape[0]
    span = LANES * peers // total
    r = pl.program_id(0)

    @pl.when(r == 0)
    def _():
        copy = pltpu.make_async_copy(far_ref, across_ref, sem)
        copy.start()
        stage[...] = pay_ref[...].astype(jnp.float32)
        tags_ref[...] = stage[pl.ds(MOST * segs, total, stride=rows), :]
        stats_ref[...] = jnp.zeros_like(stats_ref)
        copy.wait()

    lane = lax.broadcasted_iota(jnp.int32, (total, LANES), 1)
    shares = jnp.where(lane == r, 32.0, 0.0) + jnp.where(lane == GAP + r, 1.0, 0.0)
    col = jnp.sum(tags_ref[...] * shares, axis=1, keepdims=True).astype(jnp.int32) - 1
    part = jnp.concatenate(
        [stage[pl.ds(segs * r + s, total, stride=rows), :] for s in range(segs)], axis=1
    ).astype(jnp.bfloat16)
    rows_ref[0] = part
    col_wide = jnp.broadcast_to(col, (total, LANES))
    tile_of = jnp.where(lane == (col_wide & (LANES - 1)), col_wide >> 7, -1)
    sums = jnp.zeros((total, LANES), jnp.float32)
    found = jnp.zeros((total, LANES), jnp.float32)
    wide = 2 * LANES
    for c in range(0, count, wide):
        scores = nn_dot(part, across_ref[:, c : c + wide])
        for h in range(0, wide, LANES):
            tile = scores[:, h : h + LANES]
            hit = tile_of == (c + h) // LANES
            exps = jnp.where(hit, 0.0, jnp.exp(tile))
            exps_ref[0, :, c + h : c + h + LANES] = exps.astype(jnp.bfloat16)
            sums = sums + exps
            found = jnp.where(hit, tile, found)
    own = col >= 0
    target = jnp.sum(found, axis=1, keepdims=True) - LOGIT_SCALE * MARGIN
    target = jnp.where(own, target, 0.0)
    sums = jnp.sum(sums, axis=1, keepdims=True) + jnp.where(own, jnp.exp(target), 0.0)
    stats = jnp.where(lane == r, sums, stats_ref[...])
    stats_ref[...] = jnp.where(lane == GAP + r, target, stats)

    @pl.when(r == MOST - 1)
    def _():
        is_id = (lane >= 2 * GAP) & (lane < 2 * GAP + MOST)
        stats = jnp.where(is_id, tags_ref[...] - 1.0, stats_ref[...])
        brief = stats[:peers]
        for j in range(1, total // peers):
            brief = brief + pltpu.roll(stats[peers * j : peers * (j + 1)], span * j, 1)
        brief_ref[...] = brief


def partial_kernel(exps_ref, tags_ref, scaled_ref, sums_ref, hits_ref):
    total, count = exps_ref.shape[1:]
    r = pl.program_id(0)
    lane = lax.broadcasted_iota(jnp.int32, (total, LANES), 1)
    shares = jnp.where(lane == r, 32.0, 0.0) + jnp.where(lane == GAP + r, 1.0, 0.0)
    col = jnp.sum(tags_ref[...] * shares, axis=1, keepdims=True).astype(jnp.int32) - 1
    hit = lax.broadcasted_iota(jnp.int32, (1, count), 1) == col
    sums_ref[r] = nn_dot(exps_ref[0], scaled_ref[...]).astype(jnp.bfloat16)
    chosen = jnp.where(hit, 1.0, 0.0).astype(jnp.bfloat16)
    hits_ref[r] = nn_dot(chosen, scaled_ref[...]).astype(jnp.bfloat16)


def gather_kernel(brief_ref, out_ref):
    peers = brief_ref.shape[0]
    copies = out_ref.shape[0]
    groups = out_ref.shape[1] // 2
    span = LANES // groups
    fields = brief_ref[...].T
    ids = lax.broadcasted_iota(jnp.int32, (LANES, peers), 0).astype(jnp.float32)
    field = lax.broadcasted_iota(jnp.int32, (LANES, LANES), 1)
    dense = jnp.zeros((LANES, LANES), jnp.float32)
    for j in range(groups):
        total = jnp.zeros((LANES, peers), jnp.float32)
        target = jnp.zeros((LANES, peers), jnp.float32)
        for r in range(MOST):
            at = span * j + r
            hit = ids == fields[at + 2 * GAP : at + 2 * GAP + 1]
            total = total + jnp.where(hit, fields[at : at + 1], 0.0)
            target = target + jnp.where(hit, fields[at + GAP : at + GAP + 1], 0.0)
        dense = jnp.where(field == j, jnp.sum(total, axis=1, keepdims=True), dense)
        dense = jnp.where(field == groups + j, jnp.sum(target, axis=1, keepdims=True), dense)
    dense = dense.T[: 2 * groups]
    for k in range(copies):
        out_ref[k] = dense


def totals_kernel(dense_ref, brief_ref, back_ref, loss_ref):
    peers = brief_ref.shape[0]
    copies, pairs = dense_ref.shape[:2]
    groups = pairs // 2
    span = LANES // groups
    dense = dense_ref[0]
    for k in range(1, copies):
        dense = dense + dense_ref[k]
    denom = dense[:groups]
    loss_ref[...] = jnp.log(denom) - dense[groups:]
    lane = lax.broadcasted_iota(jnp.int32, (peers, LANES), 1)
    ids = pltpu.roll(brief_ref[...], LANES - 2 * GAP, 1)
    ids = jnp.clip(ids, 0.0, LANES - 1.0).astype(jnp.int32)
    back = jnp.zeros((peers, LANES), jnp.float32)
    for j in range(groups):
        row = jnp.broadcast_to(denom[j : j + 1], (peers, LANES))
        found = jnp.take_along_axis(row, ids, axis=1, mode="promise_in_bounds")
        back = jnp.where(lane // span == j, found, back)
    back_ref[...] = back


def spread(back, total):
    groups = total // back.shape[0]
    span = LANES // groups
    parts = [back]
    for j in range(1, groups):
        parts.append(pltpu.roll(back, LANES - span * j, 1))
    return jnp.concatenate(parts, axis=0)


def slot_terms(denom, tags, stats):
    gain = pltpu.roll(tags, LANES - 3 * GAP, 1)
    target = pltpu.roll(stats, LANES - GAP, 1)
    held = gain > 0.0
    factors = jnp.where(held, gain / jnp.where(held, denom, 1.0), 0.0)
    cols = 32.0 * tags + pltpu.roll(tags, LANES - GAP, 1) - 1.0
    return factors, factors * jnp.exp(target) - gain, cols


def return_kernel(back_ref, tags_ref, stats_ref, sums_ref, hits_ref, out_ref, stage, denoms):
    some = stats_ref.shape[0]
    width = sums_ref.shape[2]
    segs = width // LANES
    step = pl.program_id(0)
    mine = pl.ds(pl.multiple_of(step * some, some), some)

    @pl.when(step == 0)
    def _():
        denoms[...] = spread(back_ref[...], denoms.shape[0])

    factors, at_labels, _ = slot_terms(denoms[mine, :], tags_ref[...], stats_ref[...])
    for r in range(MOST):
        grads = factors[:, r : r + 1] * sums_ref[r, mine, :].astype(jnp.float32)
        grads = grads + at_labels[:, r : r + 1] * hits_ref[r, mine, :].astype(jnp.float32)
        for s in range(segs):
            stage[pl.ds(segs * r + s, some, stride=MOST * segs), :] = grads[
                :, LANES * s : LANES * (s + 1)
            ]
    out_ref[...] = stage[...].astype(jnp.bfloat16)


def center_grad_kernel(back_ref, exps_ref, tags_ref, stats_ref, rows_ref, centers_ref, out_ref):
    total, count = exps_ref.shape[1:]
    denom = spread(back_ref[...], total)
    factors, at_labels, cols = slot_terms(denom, tags_ref[...], stats_ref[...])
    cols = cols.astype(jnp.int32)
    unit_grad = jnp.zeros(out_ref.shape, jnp.float32)
    for r in range(MOST):
        hit = lax.broadcasted_iota(jnp.int32, (1, count), 1) == cols[:, r : r + 1]
        weights = factors[:, r : r + 1] * exps_ref[r].astype(jnp.float32)
        weights = jnp.where(hit, at_labels[:, r : r + 1], weights)
        unit_grad = unit_grad + tn_dot(weights.astype(jnp.bfloat16), rows_ref[r])
    unit_grad = LOGIT_SCALE * unit_grad
    c = centers_ref[...].astype(jnp.float32)
    length = jnp.sqrt(jnp.sum(c * c, axis=1, keepdims=True) + EPSILON)
    unit = c / length
    along = jnp.sum(unit * unit_grad, axis=1, keepdims=True)
    out_ref[...] = ((unit_grad - unit * along) / length).astype(jnp.bfloat16)


def combine_kernel(back_ref, sel_ref, far_ref, out_ref, stage, feat_ref, sem):
    samples, width = feat_ref.shape
    copy = pltpu.make_async_copy(far_ref, feat_ref, sem)
    copy.start()
    total = sel_ref.shape[1]
    segs = width // LANES
    stage[...] = back_ref[...].astype(jnp.float32)
    unit_grad = jnp.zeros((samples, width), jnp.float32)
    for r in range(MOST):
        part = jnp.concatenate(
            [stage[pl.ds(segs * r + s, total, stride=MOST * segs), :] for s in range(segs)],
            axis=1,
        ).astype(jnp.bfloat16)
        unit_grad = unit_grad + tn_dot(sel_ref[r], part)
    copy.wait()
    x = feat_ref[...].astype(jnp.float32)
    norm = jnp.sqrt(jnp.sum(x * x, axis=1, keepdims=True) + EPSILON)
    unit = x / norm
    along = jnp.sum(unit * unit_grad, axis=1, keepdims=True)
    out_ref[...] = (unit_grad - unit * along) / norm


def exchange(x, axes=AXES):
    return lax.all_to_all(x, axes, split_axis=0, concat_axis=0, tiled=True)


def place():
    return lax.axis_index("z")


def on_device(groups, features, loss_scale, blocks, label_col, block_slot, centers):
    samples, width = features.shape
    total = block_slot.shape[0]
    count = centers.shape[0]
    segs = width // LANES
    rows = MOST * segs + 2
    back_rows = MOST * segs
    bf16, f32 = jnp.bfloat16, jnp.float32
    far, here = pltpu.HBM, pltpu.VMEM
    chunks = 2
    some = total // chunks
    payload, sel = call(
        "dispatch",
        dispatch_kernel,
        tuple(
            away(x)
            for x in (
                features,
                blocks.T,
                label_col.reshape(1, samples),
                loss_scale.reshape(1, samples),
                block_slot.reshape(1, total),
            )
        ),
        (far((total * rows, LANES), bf16), far((MOST, total, samples), bf16)),
        [here((total * rows, LANES), f32)],
    )
    payload_in = exchange(payload.reshape(total, rows // 2, 2, LANES)).reshape(total * rows, LANES)
    scaled, across = call(
        "normalize",
        centers_kernel,
        (centers,),
        (far((count, width), bf16), far((width, count), bf16)),
    )
    peers = total // groups
    rows_x, exps, tags, stats, brief = call(
        "scores",
        scores_kernel,
        (near(payload_in), away(across)),
        (
            far((MOST, total, width), bf16),
            far((MOST, total, count), bf16),
            far((total, LANES), f32),
            far((total, LANES), f32),
            far((peers, LANES), f32),
        ),
        [
            here((total * rows, LANES), f32),
            here((width, count), bf16),
            pltpu.SemaphoreType.DMA,
        ],
        grid=(MOST,),
        ins=[WHOLE, AWAY],
        to=(
            block((1, total, width), lambda r: (r, 0, 0)),
            block((1, total, count), lambda r: (r, 0, 0)),
            block((total, LANES), lambda r: (0, 0)),
            block((total, LANES), lambda r: (0, 0)),
            block((peers, LANES), lambda r: (0, 0)),
        ),
    )
    brief_in = exchange(brief.reshape(peers, 1, LANES), PLANE).reshape(peers, LANES)
    (dense,) = call(
        "gather", gather_kernel, (near(brief_in),), (far((groups, 2 * groups, LANES), f32),)
    )
    dense_in = exchange(dense, ("z",))
    denoms, losses = call(
        "totals",
        totals_kernel,
        (near(dense_in), near(brief_in)),
        (far((peers, LANES), f32), far((groups, LANES), f32)),
    )
    denoms_in = exchange(denoms.reshape(peers, 1, LANES), PLANE).reshape(peers, LANES)
    loss = lax.dynamic_index_in_dim(losses, place(), 0, keepdims=False)
    sums, hits = call(
        "partial",
        partial_kernel,
        (away(exps), away(tags), away(scaled)),
        (here((MOST, total, width), bf16), here((MOST, total, width), bf16)),
        grid=(MOST,),
        ins=[block((1, total, count), lambda r: (r, 0, 0)), WHOLE, WHOLE],
    )
    (returned,) = call(
        "returned",
        return_kernel,
        (near(denoms_in), away(tags), away(stats), near(sums), near(hits)),
        (far((total * back_rows, LANES), bf16),),
        [here((some * back_rows, LANES), f32), here((total, LANES), f32)],
        grid=(chunks,),
        ins=[
            WHOLE,
            block((some, LANES), lambda d: (d, 0)),
            block((some, LANES), lambda d: (d, 0)),
            WHOLE,
            WHOLE,
        ],
        to=(block((some * back_rows, LANES), lambda d: (d, 0)),),
    )
    back = exchange(returned.reshape(total, MOST, segs, LANES)).reshape(total * back_rows, LANES)
    (center_grad,) = call(
        "center_grad",
        center_grad_kernel,
        (near(denoms_in), away(exps), away(tags), away(stats), away(rows_x), away(centers)),
        (far((count, width), bf16),),
    )
    (feature_grad,) = call(
        "combine",
        combine_kernel,
        (near(back), near(sel), away(features)),
        (far((samples, width), f32),),
        [
            here((total * back_rows, LANES), f32),
            here((samples, width), bf16),
            pltpu.SemaphoreType.DMA,
        ],
        ins=[WHOLE, WHOLE, AWAY],
    )
    return (loss, feature_grad, center_grad)


def solution(mesh):
    groups = 8
    split = (groups, mesh.shape["dp"] // groups // 2, 2, mesh.shape["grp"])
    mesh = Mesh(mesh.devices.reshape(split), AXES)
    placed = (
        P(AXES, None),
        P(AXES),
        P(AXES, None),
        P(AXES),
        P(),
        P(AXES, None),
    )
    return jax.shard_map(
        functools.partial(on_device, groups),
        mesh=mesh,
        in_specs=placed,
        out_specs=(P(AXES), P(AXES, None), P(AXES, None)),
        check_vma=False,
    )
```

```python
import functools

import jax
import jax.numpy as jnp
from jax import lax
from jax.experimental import pallas as pl
from jax.experimental.pallas import tpu as pltpu
from jax.sharding import Mesh
from jax.sharding import PartitionSpec as P

BLOCK = 1024
MOST = 3
GAP = 4
LANES = 128
MARGIN = 0.35
LOGIT_SCALE = 64.0
EPSILON = 1e-06
AXES = ("z", "y", "core", "grp")
PLANE = ("y", "core", "grp")

MIB = 1024 * 1024


def nt_dot(a, b):
    return lax.dot_general(a, b, (((1,), (1,)), ((), ())), preferred_element_type=jnp.float32)


def tn_dot(a, b):
    return lax.dot_general(a, b, (((0,), (0,)), ((), ())), preferred_element_type=jnp.float32)


def nn_dot(a, b):
    return jnp.dot(a, b, preferred_element_type=jnp.float32)


WHOLE = pl.BlockSpec(memory_space=pltpu.VMEM)


AWAY = pl.BlockSpec(memory_space=pl.ANY)


def block(shape, place):
    return pl.BlockSpec(shape, place)


def call(name, kernel, args, outs, scratch=(), grid=(), ins=None, to=None, limit=28):
    return pl.pallas_call(
        kernel,
        out_shape=tuple(outs),
        grid=grid,
        in_specs=ins or [WHOLE] * len(args),
        out_specs=to or tuple(WHOLE for _ in outs),
        scratch_shapes=list(scratch),
        compiler_params=pltpu.CompilerParams(vmem_limit_bytes=limit * MIB),
        name=name,
    )(*args)


def near(x):
    return pltpu.with_memory_space_constraint(x, pltpu.VMEM)


def away(x):
    return pltpu.with_memory_space_constraint(x, pltpu.HBM)


def dispatch_kernel(
    feat_ref, blocks_ref, label_ref, gain_ref, slot_ref, pay_ref, sel_ref, stage
):
    samples, width = feat_ref.shape
    total = slot_ref.shape[1]
    segs = width // LANES
    rows = MOST * segs + 2
    x = feat_ref[...].astype(jnp.float32)
    norm = jnp.sqrt(jnp.sum(x * x, axis=1, keepdims=True) + EPSILON)
    normed = (x / norm).astype(jnp.bfloat16)
    named_by = blocks_ref[...]
    block_iota = lax.broadcasted_iota(jnp.int32, (total, samples), 0)
    own = block_iota == named_by[0:1]
    named = own
    for k in range(1, blocks_ref.shape[0]):
        named = named | (block_iota == named_by[k : k + 1])
    both = jnp.concatenate([named.astype(jnp.float32), own.astype(jnp.float32)], axis=1)
    one_hot = (lax.broadcasted_iota(jnp.int32, (total, total), 0) == slot_ref[...]).astype(
        jnp.float32
    ).astype(jnp.bfloat16)
    both_at = nn_dot(one_hot, both.astype(jnp.bfloat16))
    named_at = both_at[:, :samples]
    own_at = both_at[:, samples:]
    before = (
        lax.broadcasted_iota(jnp.int32, (samples, samples), 0)
        < lax.broadcasted_iota(jnp.int32, (samples, samples), 1)
    ).astype(jnp.float32).astype(jnp.bfloat16)
    rank = nn_dot(named_at.astype(jnp.bfloat16), before)
    label = label_ref[...].astype(jnp.float32) + 1.0
    high = jnp.floor(label * (1.0 / 32.0))
    low = label - 32.0 * high
    gain = gain_ref[...].astype(jnp.float32)
    field = lax.broadcasted_iota(jnp.int32, (LANES, samples), 0)
    ids = lax.broadcasted_iota(jnp.int32, (LANES, samples), 1).astype(jnp.float32) + 1.0
    tags = jnp.zeros((total, LANES), jnp.float32)
    for r in range(MOST):
        sel = jnp.where(rank == float(r), named_at, 0.0)
        sel_bf = sel.astype(jnp.bfloat16)
        sel_ref[r] = sel_bf
        picked = nn_dot(sel_bf, normed)
        for s in range(segs):
            stage[pl.ds(segs * r + s, total, stride=rows), :] = picked[
                :, LANES * s : LANES * (s + 1)
            ]
        own_tags = jnp.where(field == r, high, jnp.where(field == GAP + r, low, 0.0))
        all_tags = jnp.where(field == 2 * GAP + r, ids, jnp.where(field == 3 * GAP + r, gain, 0.0))
        tags = tags + nt_dot((sel * own_at).astype(jnp.bfloat16), own_tags.astype(jnp.bfloat16))
        tags = tags + nt_dot(sel_bf, all_tags.astype(jnp.bfloat16))
    stage[pl.ds(MOST * segs, total, stride=rows), :] = tags
    stage[pl.ds(MOST * segs + 1, total, stride=rows), :] = jnp.zeros_like(tags)
    pay_ref[...] = stage[...].astype(jnp.bfloat16)


def centers_kernel(centers_ref, scaled_ref, across_ref):
    c = centers_ref[...].astype(jnp.float32)
    length = jnp.sqrt(jnp.sum(c * c, axis=1, keepdims=True) + EPSILON)
    scaled = LOGIT_SCALE * (c / length).astype(jnp.bfloat16).astype(jnp.float32)
    scaled_ref[...] = scaled.astype(jnp.bfloat16)
    across_ref[...] = scaled.T.astype(jnp.bfloat16)


def scores_kernel(
    pay_ref, far_ref, rows_ref, exps_ref, tags_ref, stats_ref, brief_ref, stage, across_ref, sem
):
    width, count = across_ref.shape
    segs = width // LANES
    rows = MOST * segs + 2
    total = pay_ref.shape[0] // rows
    peers = brief_ref.shape[0]
    span = LANES * peers // total
    r = pl.program_id(0)

    @pl.when(r == 0)
    def _():
        copy = pltpu.make_async_copy(far_ref, across_ref, sem)
        copy.start()
        stage[...] = pay_ref[...].astype(jnp.float32)
        tags_ref[...] = stage[pl.ds(MOST * segs, total, stride=rows), :]
        stats_ref[...] = jnp.zeros_like(stats_ref)
        copy.wait()

    lane = lax.broadcasted_iota(jnp.int32, (total, LANES), 1)
    shares = jnp.where(lane == r, 32.0, 0.0) + jnp.where(lane == GAP + r, 1.0, 0.0)
    col = jnp.sum(tags_ref[...] * shares, axis=1, keepdims=True).astype(jnp.int32) - 1
    part = jnp.concatenate(
        [stage[pl.ds(segs * r + s, total, stride=rows), :] for s in range(segs)], axis=1
    ).astype(jnp.bfloat16)
    rows_ref[0] = part
    col_wide = jnp.broadcast_to(col, (total, LANES))
    tile_of = jnp.where(lane == (col_wide & (LANES - 1)), col_wide >> 7, -1)
    sums = jnp.zeros((total, LANES), jnp.float32)
    found = jnp.zeros((total, LANES), jnp.float32)
    wide = 2 * LANES
    for c in range(0, count, wide):
        scores = nn_dot(part, across_ref[:, c : c + wide])
        for h in range(0, wide, LANES):
            tile = scores[:, h : h + LANES]
            hit = tile_of == (c + h) // LANES
            exps = jnp.where(hit, 0.0, jnp.exp(tile))
            exps_ref[0, :, c + h : c + h + LANES] = exps.astype(jnp.bfloat16)
            sums = sums + exps
            found = jnp.where(hit, tile, found)
    own = col >= 0
    target = jnp.sum(found, axis=1, keepdims=True) - LOGIT_SCALE * MARGIN
    target = jnp.where(own, target, 0.0)
    sums = jnp.sum(sums, axis=1, keepdims=True) + jnp.where(own, jnp.exp(target), 0.0)
    stats = jnp.where(lane == r, sums, stats_ref[...])
    stats_ref[...] = jnp.where(lane == GAP + r, target, stats)

    @pl.when(r == MOST - 1)
    def _():
        is_id = (lane >= 2 * GAP) & (lane < 2 * GAP + MOST)
        stats = jnp.where(is_id, tags_ref[...] - 1.0, stats_ref[...])
        brief = stats[:peers]
        for j in range(1, total // peers):
            brief = brief + pltpu.roll(stats[peers * j : peers * (j + 1)], span * j, 1)
        brief_ref[...] = brief


def partial_kernel(exps_ref, tags_ref, scaled_ref, sums_ref, hits_ref):
    total, count = exps_ref.shape[1:]
    r = pl.program_id(0)
    lane = lax.broadcasted_iota(jnp.int32, (total, LANES), 1)
    shares = jnp.where(lane == r, 32.0, 0.0) + jnp.where(lane == GAP + r, 1.0, 0.0)
    col = jnp.sum(tags_ref[...] * shares, axis=1, keepdims=True).astype(jnp.int32) - 1
    sums_ref[r] = nn_dot(exps_ref[0], scaled_ref[...]).astype(jnp.bfloat16)
    col_wide = jnp.broadcast_to(col, (total, LANES))
    tile_of = jnp.where(lane == (col_wide & (LANES - 1)), col_wide >> 7, -1)
    tiles = [jnp.where(tile_of == t, 1.0, 0.0) for t in range(count // LANES)]
    chosen = jnp.concatenate(tiles, axis=1).astype(jnp.bfloat16)
    hits_ref[r] = nn_dot(chosen, scaled_ref[...]).astype(jnp.bfloat16)


def gather_kernel(brief_ref, out_ref):
    peers = brief_ref.shape[0]
    copies = out_ref.shape[0]
    groups = out_ref.shape[1] // 2
    span = LANES // groups
    fields = brief_ref[...].T
    ids = lax.broadcasted_iota(jnp.int32, (LANES, peers), 0).astype(jnp.float32)
    field = lax.broadcasted_iota(jnp.int32, (LANES, LANES), 1)
    dense = jnp.zeros((LANES, LANES), jnp.float32)
    for j in range(groups):
        total = jnp.zeros((LANES, peers), jnp.float32)
        target = jnp.zeros((LANES, peers), jnp.float32)
        for r in range(MOST):
            at = span * j + r
            hit = ids == fields[at + 2 * GAP : at + 2 * GAP + 1]
            total = total + jnp.where(hit, fields[at : at + 1], 0.0)
            target = target + jnp.where(hit, fields[at + GAP : at + GAP + 1], 0.0)
        dense = jnp.where(field == j, jnp.sum(total, axis=1, keepdims=True), dense)
        dense = jnp.where(field == groups + j, jnp.sum(target, axis=1, keepdims=True), dense)
    dense = dense.T[: 2 * groups]
    for k in range(copies):
        out_ref[k] = dense


def totals_kernel(dense_ref, brief_ref, back_ref, loss_ref):
    peers = brief_ref.shape[0]
    copies, pairs = dense_ref.shape[:2]
    groups = pairs // 2
    span = LANES // groups
    dense = dense_ref[0]
    for k in range(1, copies):
        dense = dense + dense_ref[k]
    denom = dense[:groups]
    loss_ref[...] = jnp.log(denom) - dense[groups:]
    lane = lax.broadcasted_iota(jnp.int32, (peers, LANES), 1)
    ids = pltpu.roll(brief_ref[...], LANES - 2 * GAP, 1)
    ids = jnp.clip(ids, 0.0, LANES - 1.0).astype(jnp.int32)
    back = jnp.zeros((peers, LANES), jnp.float32)
    for j in range(groups):
        row = jnp.broadcast_to(denom[j : j + 1], (peers, LANES))
        found = jnp.take_along_axis(row, ids, axis=1, mode="promise_in_bounds")
        back = jnp.where(lane // span == j, found, back)
    back_ref[...] = back


def spread(back, total):
    groups = total // back.shape[0]
    span = LANES // groups
    parts = [back]
    for j in range(1, groups):
        parts.append(pltpu.roll(back, LANES - span * j, 1))
    return jnp.concatenate(parts, axis=0)


def slot_terms(denom, tags, stats):
    gain = pltpu.roll(tags, LANES - 3 * GAP, 1)
    target = pltpu.roll(stats, LANES - GAP, 1)
    held = gain > 0.0
    factors = jnp.where(held, gain / jnp.where(held, denom, 1.0), 0.0)
    cols = 32.0 * tags + pltpu.roll(tags, LANES - GAP, 1) - 1.0
    return factors, factors * jnp.exp(target) - gain, cols


def return_kernel(back_ref, tags_ref, stats_ref, sums_ref, hits_ref, out_ref, stage, denoms):
    some = stats_ref.shape[0]
    width = sums_ref.shape[2]
    segs = width // LANES
    step = pl.program_id(0)
    mine = pl.ds(pl.multiple_of(step * some, some), some)

    @pl.when(step == 0)
    def _():
        denoms[...] = spread(back_ref[...], denoms.shape[0])

    factors, at_labels, _ = slot_terms(denoms[mine, :], tags_ref[...], stats_ref[...])
    for r in range(MOST):
        grads = factors[:, r : r + 1] * sums_ref[r, mine, :].astype(jnp.float32)
        grads = grads + at_labels[:, r : r + 1] * hits_ref[r, mine, :].astype(jnp.float32)
        for s in range(segs):
            stage[pl.ds(segs * r + s, some, stride=MOST * segs), :] = grads[
                :, LANES * s : LANES * (s + 1)
            ]
    out_ref[...] = stage[...].astype(jnp.bfloat16)


def center_grad_kernel(back_ref, exps_ref, tags_ref, stats_ref, rows_ref, centers_ref, out_ref):
    total, count = exps_ref.shape[1:]
    denom = spread(back_ref[...], total)
    factors, at_labels, cols = slot_terms(denom, tags_ref[...], stats_ref[...])
    cols = cols.astype(jnp.int32)
    unit_grad = jnp.zeros(out_ref.shape, jnp.float32)
    for r in range(MOST):
        hit = lax.broadcasted_iota(jnp.int32, (1, count), 1) == cols[:, r : r + 1]
        weights = factors[:, r : r + 1] * exps_ref[r].astype(jnp.float32)
        weights = jnp.where(hit, at_labels[:, r : r + 1], weights)
        unit_grad = unit_grad + tn_dot(weights.astype(jnp.bfloat16), rows_ref[r])
    unit_grad = LOGIT_SCALE * unit_grad
    c = centers_ref[...].astype(jnp.float32)
    length = jnp.sqrt(jnp.sum(c * c, axis=1, keepdims=True) + EPSILON)
    unit = c / length
    along = jnp.sum(unit * unit_grad, axis=1, keepdims=True)
    out_ref[...] = ((unit_grad - unit * along) / length).astype(jnp.bfloat16)


def combine_kernel(back_ref, sel_ref, far_ref, out_ref, stage, feat_ref, sem):
    samples, width = feat_ref.shape
    copy = pltpu.make_async_copy(far_ref, feat_ref, sem)
    copy.start()
    total = sel_ref.shape[1]
    segs = width // LANES
    stage[...] = back_ref[...].astype(jnp.float32)
    unit_grad = jnp.zeros((samples, width), jnp.float32)
    for r in range(MOST):
        part = jnp.concatenate(
            [stage[pl.ds(segs * r + s, total, stride=MOST * segs), :] for s in range(segs)],
            axis=1,
        ).astype(jnp.bfloat16)
        unit_grad = unit_grad + tn_dot(sel_ref[r], part)
    copy.wait()
    x = feat_ref[...].astype(jnp.float32)
    norm = jnp.sqrt(jnp.sum(x * x, axis=1, keepdims=True) + EPSILON)
    unit = x / norm
    along = jnp.sum(unit * unit_grad, axis=1, keepdims=True)
    out_ref[...] = (unit_grad - unit * along) / norm


def exchange(x, axes=AXES):
    return lax.all_to_all(x, axes, split_axis=0, concat_axis=0, tiled=True)


def place():
    return lax.axis_index("z")


def on_device(groups, features, loss_scale, blocks, label_col, block_slot, centers):
    samples, width = features.shape
    total = block_slot.shape[0]
    count = centers.shape[0]
    segs = width // LANES
    rows = MOST * segs + 2
    back_rows = MOST * segs
    bf16, f32 = jnp.bfloat16, jnp.float32
    far, here = pltpu.HBM, pltpu.VMEM
    chunks = 2
    some = total // chunks
    payload, sel = call(
        "dispatch",
        dispatch_kernel,
        tuple(
            away(x)
            for x in (
                features,
                blocks.T,
                label_col.reshape(1, samples),
                loss_scale.reshape(1, samples),
                block_slot.reshape(1, total),
            )
        ),
        (far((total * rows, LANES), bf16), far((MOST, total, samples), bf16)),
        [here((total * rows, LANES), f32)],
    )
    payload_in = exchange(payload.reshape(total, rows // 2, 2, LANES)).reshape(total * rows, LANES)
    scaled, across = call(
        "normalize",
        centers_kernel,
        (centers,),
        (far((count, width), bf16), far((width, count), bf16)),
    )
    peers = total // groups
    rows_x, exps, tags, stats, brief = call(
        "scores",
        scores_kernel,
        (near(payload_in), away(across)),
        (
            far((MOST, total, width), bf16),
            far((MOST, total, count), bf16),
            far((total, LANES), f32),
            far((total, LANES), f32),
            far((peers, LANES), f32),
        ),
        [
            here((total * rows, LANES), f32),
            here((width, count), bf16),
            pltpu.SemaphoreType.DMA,
        ],
        grid=(MOST,),
        ins=[WHOLE, AWAY],
        to=(
            block((1, total, width), lambda r: (r, 0, 0)),
            block((1, total, count), lambda r: (r, 0, 0)),
            block((total, LANES), lambda r: (0, 0)),
            block((total, LANES), lambda r: (0, 0)),
            block((peers, LANES), lambda r: (0, 0)),
        ),
    )
    brief_in = exchange(brief.reshape(peers, 1, LANES), PLANE).reshape(peers, LANES)
    (dense,) = call(
        "gather", gather_kernel, (near(brief_in),), (far((groups, 2 * groups, LANES), f32),)
    )
    dense_in = exchange(dense, ("z",))
    denoms, losses = call(
        "totals",
        totals_kernel,
        (near(dense_in), near(brief_in)),
        (far((peers, LANES), f32), far((groups, LANES), f32)),
    )
    denoms_in = exchange(denoms.reshape(peers, 1, LANES), PLANE).reshape(peers, LANES)
    loss = lax.dynamic_index_in_dim(losses, place(), 0, keepdims=False)
    sums, hits = call(
        "partial",
        partial_kernel,
        (away(exps), away(tags), away(scaled)),
        (here((MOST, total, width), bf16), here((MOST, total, width), bf16)),
        grid=(MOST,),
        ins=[block((1, total, count), lambda r: (r, 0, 0)), WHOLE, WHOLE],
    )
    (returned,) = call(
        "returned",
        return_kernel,
        (near(denoms_in), away(tags), away(stats), near(sums), near(hits)),
        (far((total * back_rows, LANES), bf16),),
        [here((some * back_rows, LANES), f32), here((total, LANES), f32)],
        grid=(chunks,),
        ins=[
            WHOLE,
            block((some, LANES), lambda d: (d, 0)),
            block((some, LANES), lambda d: (d, 0)),
            WHOLE,
            WHOLE,
        ],
        to=(block((some * back_rows, LANES), lambda d: (d, 0)),),
    )
    back = exchange(returned.reshape(total, MOST, segs, LANES)).reshape(total * back_rows, LANES)
    (center_grad,) = call(
        "center_grad",
        center_grad_kernel,
        (near(denoms_in), away(exps), away(tags), away(stats), away(rows_x), away(centers)),
        (far((count, width), bf16),),
    )
    (feature_grad,) = call(
        "combine",
        combine_kernel,
        (near(back), near(sel), away(features)),
        (far((samples, width), f32),),
        [
            here((total * back_rows, LANES), f32),
            here((samples, width), bf16),
            pltpu.SemaphoreType.DMA,
        ],
        ins=[WHOLE, WHOLE, AWAY],
    )
    return (loss, feature_grad, center_grad)


def solution(mesh):
    groups = 8
    split = (groups, mesh.shape["dp"] // groups // 2, 2, mesh.shape["grp"])
    mesh = Mesh(mesh.devices.reshape(split), AXES)
    placed = (
        P(AXES, None),
        P(AXES),
        P(AXES, None),
        P(AXES),
        P(),
        P(AXES, None),
    )
    return jax.shard_map(
        functools.partial(on_device, groups),
        mesh=mesh,
        in_specs=placed,
        out_specs=(P(AXES), P(AXES, None), P(AXES, None)),
        check_vma=False,
    )
```
